512 devices in a mesh: feat: 64 (over x, z_hi, y, core), tok: 8 (over z_lo).
Axes of the slice: x: 4, y: 4, z: 16 (z_hi: 2, z_lo: 8; z = z_hi * 8 + z_lo), core: 2. Of those that a mesh axis runs over, the one named last changes fastest.
Arguments:
- features: bfloat16 [1024, 131072], P('tok', 'feat'), may hold values from -6 to 6
- signs: int32 [131072], P('feat'), may hold values from -1 to 1, as said below
- columns: int32 [1024], replicated, may hold values from 0 to 131071, as said below
- labels: int32 [1024, 1], P('tok'), may hold values from 0 to 31; in each aligned block of 128 rows (0 to 127, 128 to 255, ...) at most 8 rows name the same one
Outputs:
- gram: float32 [32, 1024, 1024], P('tok', 'feat')
The draws below stay inside these ranges and needn't reach their ends.
Inputs may be any that keep to these rules, and one draw needn't show every extreme that they name: `signs`: every entry is -1 or 1. `columns`: the 1024 indices are distinct. `labels`: among the rows of one device no concept appears more than 8 times.
All inputs are finite; a program needn't handle non-finite values.
Results may differ from the reference program's by a relative error of at most 0.004.
Values may be sent and summed in bfloat16 or wider, within the bound.
A program may use at most 64 MiB of HBM per device.

```python
import math
import jax
import jax.numpy as jnp
import numpy as np
from jax import lax

F = 131072
K = 1024
C = 32
TOK_DEV = 128
TOKENS = 1024
MOST = 8


def draw_signs(key, part):
    return (2 * jax.random.randint(key, (F,), 0, 2) - 1).astype(jnp.int32)


def draw_columns(key, part):
    return jax.random.permutation(key, F)[:K].astype(jnp.int32)


def levels(own_key, extent, cuts, smallest, largest):
    def one(axis_at, parts):
        draws = jax.random.uniform(jax.random.fold_in(jax.random.fold_in(own_key, 6), axis_at), (parts,), jnp.float32, smallest / len(cuts), largest / len(cuts))
        return jnp.repeat(jnp.exp(draws), extent[axis_at] // parts).reshape((-1,) + (1,) * (len(extent) - axis_at - 1))

    factor_of = one(*cuts[0])
    for cut in cuts[1:]:
        factor_of = factor_of * one(*cut)
    return factor_of


def assign_block(stream_key, own, number, rows, amount, top, reach, skew):
    sequence = jax.random.permutation(stream_key, amount)
    heavy_load, usual = portions_of(amount, rows * top, reach, skew, True), portions_of(amount, rows * top, reach, skew, False)
    places = jnp.arange(amount)

    def named(sizes, offset_by):
        used = int((sizes > 0).sum())
        fixed = max(1, used // 4)
        shifted = fixed + (places - fixed + offset_by * (used - fixed)) % max(1, amount - fixed)
        return jnp.zeros((amount,), jnp.int32).at[sequence[jnp.where(places < fixed, places, shifted)]].set(jnp.asarray(sizes, jnp.int32))

    sizes = jnp.where(number % 4 == 0, named(heavy_load, number // 4), named(usual, number - number // 4 - 1))
    mixed = jax.random.permutation(jax.random.fold_in(own, 3), amount)
    source_of, sink = mixed[0:amount // 2 * 2:2], mixed[1:amount // 2 * 2:2]
    slack = jnp.minimum(sizes[source_of] - 1, reach - sizes[sink]) // 2
    slack = jnp.where((source_of == sequence[0]) | (sink == sequence[0]) | (sizes[sink] == 0), 0, jnp.maximum(slack, 0))
    shifted = jax.random.randint(jax.random.fold_in(own, 4), (amount // 2,), 0, 1 << 20) % (slack + 1)
    sizes = sizes.at[source_of].add(-shifted).at[sink].add(shifted)
    items = jnp.searchsorted(jnp.cumsum(sizes), jnp.arange(rows * top), side="right").astype(jnp.int32)
    table = items.reshape(top, rows).T
    table = table[jax.random.permutation(jax.random.fold_in(own, 1), rows)]
    offset_by = jax.random.randint(jax.random.fold_in(own, 2), (rows, 1), 0, top)
    return jnp.take_along_axis(table, (jnp.arange(top)[None, :] + offset_by) % top, axis=1)


def portions_of(number_of, total, reach, slope, full):
    portions = [(1 << 20) // math.isqrt(standing ** slope) + 1 for standing in range(1, number_of + 1)]
    largest = reach if full else min(reach, max(-(-total // number_of), total * portions[0] // sum(portions)))
    least = 1 if total - largest >= number_of - 1 else 0
    given, surplus = [largest] + [least] * (number_of - 1), total - largest - least * (number_of - 1)
    while surplus > 0:
        candidates = [i for i in range(1, number_of) if given[i] < largest] or [i for i in range(1, number_of) if given[i] < reach]
        mass, budget = sum([portions[i] for i in candidates]), surplus
        for i in candidates:
            addition = min(reach - given[i], max(1, budget * portions[i] // mass), surplus)
            given[i] = given[i] + addition
            surplus = surplus - addition
    return np.array(given)


def gaussian(rng, shape, spread, most, split=(), held_as=jnp.bfloat16):
    values = jax.random.normal(rng, shape, jnp.float32) * spread
    if len(split) > 0:
        values = levels(rng, shape, split, -0.22, 0.18) * values
    return jnp.clip(values, min=-most, max=most).astype(held_as)


def setup_inputs(seed: int = 0) -> dict:
    arg_keys = jax.random.split(jax.random.key(seed), 5)
    features = gaussian(arg_keys[0], (TOKENS, F), 1.0, 6.0, ((0, 8), (1, 64)))
    signs = draw_signs(jax.random.fold_in(arg_keys[4], 71), 0)
    columns = draw_columns(jax.random.fold_in(arg_keys[4], 71), 0)
    labels_keys = jax.random.split(jax.random.fold_in(arg_keys[3], 1), TOKENS // TOK_DEV)
    labels_turns = jax.random.permutation(jax.random.fold_in(arg_keys[3], 3), TOKENS // TOK_DEV)
    labels = jax.vmap(lambda own, number: assign_block(jax.random.fold_in(arg_keys[3], 2), own, number, TOK_DEV, C, 1, MOST, 0))(labels_keys, labels_turns).reshape((TOKENS, 1))
    return {"features": features, "signs": signs, "columns": columns, "labels": labels}


def bit_parity(number, bit_count):
    total = jnp.zeros_like(number)
    for position in range(bit_count):
        total = total ^ number >> position & 1
    return total

def sylvester(order, dtype):
    index = lax.iota(jnp.int32, order)
    parity = bit_parity(index[:, None] & index[None, :], order.bit_length())
    return (1 - 2 * parity).astype(dtype)

def reference(features, signs, columns, labels):
    total_rows = features.shape[0]
    width = features.shape[1]
    blocks = width // 128
    table = sylvester(128, jnp.bfloat16)
    low_part = columns % 128
    high_part = columns // 128
    outer = lax.iota(jnp.int32, blocks)
    parity = bit_parity(high_part[:, None] & outer[None, :], blocks.bit_length())
    high_sign = (1 - 2 * parity).astype(jnp.float32)
    scale = 1.0 / math.sqrt(width)
    signed = features * signs.astype(jnp.bfloat16)[None, :]
    step_rows = math.gcd(total_rows, 32)
    flat_labels = labels[:, 0]

    def one_block(rows):
        inner = jnp.dot(rows.reshape(step_rows * blocks, 128), table, preferred_element_type=jnp.float32)
        inner = inner.reshape(step_rows, blocks, 128)
        picked = jnp.take(inner, low_part, axis=2)
        mixed = jnp.einsum('bnk,kn->bk', picked, high_sign, precision=lax.Precision.HIGHEST)
        return (mixed * scale).astype(jnp.bfloat16)
    sketch = lax.map(one_block, signed.reshape(total_rows // step_rows, step_rows, width))
    sketch = sketch.reshape(total_rows, columns.shape[0]).astype(jnp.float32)
    factor = C / total_rows

    def one_concept(concept):
        chosen = (flat_labels == concept).astype(jnp.float32)
        return jnp.dot((sketch * chosen[:, None]).T, sketch, precision=lax.Precision.HIGHEST) * factor
    return lax.map(one_concept, lax.iota(jnp.int32, C))
```

```python
import math

import jax
import jax.numpy as jnp
from jax import lax
from jax.experimental import pallas as pl
from jax.experimental.pallas import tpu as pltpu
from jax.sharding import PartitionSpec as P

C = 32
MESH = pl.DeviceIdType.MESH
NX, NH, NY, NC, NG = 4, 2, 4, 2, 8
NXY = NX * NY
NZ = NH * NG


def kernel(x_ref, sg_ref, col_ref, lab_ref, out_ref, xs, s, y, r1, r2, fold, r3, g,
           send1, recv1, send2, recv2, send3, recv3, send4, recv4, send5, recv5):
    f = lax.axis_index("feat")
    tok = lax.axis_index("tok")
    core = f % NC
    py = f // NC % NY
    zh = f // (NC * NY) % NH
    px = f // (NC * NY * NH)
    xy = px * NY + py
    plane = zh * NG + tok

    def feat_of(qx, qh, qy, qc):
        return ((qx * NH + qh) * NY + qy) * NC + qc

    sibling = {"feat": feat_of(px, zh, py, 1 - core), "tok": tok}

    def xy_at(d):
        return (px + d // NY) % NX, (py + d % NY) % NY

    def xy_device(d):
        qx, qy = xy_at(d)
        return {"feat": feat_of(qx, zh, qy, core), "tok": tok}

    def z_device(d):
        other = (plane + d) % NZ
        return {"feat": feat_of(px, other // NG, py, core), "tok": other % NG}

    barrier = pltpu.get_barrier_semaphore()
    pl.semaphore_signal(barrier, inc=1, device_id=sibling, device_id_type=MESH)
    for d in range(1, NXY):
        pl.semaphore_signal(barrier, inc=1, device_id=xy_device(d), device_id_type=MESH)
    for d in range(1, NZ):
        pl.semaphore_signal(barrier, inc=1, device_id=z_device(d), device_id_type=MESH)

    xs[...] = x_ref[...] * sg_ref[...].astype(jnp.float32).astype(jnp.bfloat16)
    lane = lax.broadcasted_iota(jnp.int32, (128, 128), 1)

    def chunk(i):
        c = jnp.broadcast_to(col_ref[pl.ds(i, 1), :], (128, 128)).T
        v = (c & lane) ^ (c >> 11 & f)
        v = v ^ v >> 4
        v = v ^ v >> 2
        v = v ^ v >> 1
        parts = [(1 - 2 * (v & 1)).astype(jnp.float32).astype(jnp.bfloat16)]
        for bit in range(4):
            flip = (1 - 2 * (c >> 7 + bit & 1)).astype(jnp.float32).astype(jnp.bfloat16)
            parts = parts + [part * flip for part in parts]
        for block in range(16):
            s[:, 128 * block:128 * block + 128] = parts[block]
        found = lax.dot_general(s[...], xs[...], (((1,), (1,)), ((), ())), preferred_element_type=jnp.float32)
        y[pl.ds(4 * i, 4)] = found.reshape(4, 32, 128)

    @pl.loop(0, 4)
    def _(n):
        chunk(4 * (1 - core) + n)

    pl.semaphore_wait(barrier, 1 + (NXY - 1) + (NZ - 1))
    pair = pltpu.make_async_remote_copy(
        src_ref=y.at[pl.ds(NXY * (1 - core), NXY)], dst_ref=r1, send_sem=send1, recv_sem=recv1,
        device_id=sibling, device_id_type=MESH)
    pair.start()

    @pl.loop(0, 4)
    def _(n):
        chunk(4 * core + n)

    row = jnp.broadcast_to(lab_ref[...], (128, 128))
    col = row.T
    above = lax.broadcasted_iota(jnp.int32, (128, 128), 0)
    earlier = jnp.where((row == col) & (lane < above), 1.0, 0.0)
    rank = jnp.sum(earlier, axis=1, keepdims=True)
    slot = col.astype(jnp.float32) * 8.0 + rank
    within = (lane % 32).astype(jnp.float32)
    spread = jnp.concatenate(
        [jnp.where(slot == within + 32.0 * q, 1.0, 0.0).astype(jnp.bfloat16) for q in range(NG)], axis=1)

    pair.wait_recv()
    out2 = []
    for d in range(1, NXY):
        qx, qy = xy_at(d)
        there = qx * NY + qy
        mine = NXY * core + there
        y[mine] = y[mine] + r1[there]
        copy = pltpu.make_async_remote_copy(
            src_ref=y.at[mine], dst_ref=r2.at[d - 1], send_sem=send2.at[d - 1], recv_sem=recv2.at[d - 1],
            device_id=xy_device(d), device_id_type=MESH)
        copy.start()
        out2.append(copy)
    total = y[NXY * core + xy] + r1[xy]
    for d in range(1, NXY):
        out2[d - 1].wait_recv()
        total = total + r2[d - 1]

    hi = total.astype(jnp.bfloat16)
    rest = total - hi.astype(jnp.float32)
    mid = rest.astype(jnp.bfloat16)
    low = (rest - mid.astype(jnp.float32)).astype(jnp.bfloat16)
    picked = jnp.dot(jnp.concatenate([hi, mid, low], axis=0), spread, preferred_element_type=jnp.float32)
    picked = picked[0:32] + picked[32:64] + picked[64:96]
    quarter = lax.broadcasted_iota(jnp.int32, (8, 128), 1) // 32
    for q in range(NG):
        tile = picked[0:8, 128 * q:128 * q + 128]
        for k in range(1, 4):
            tile = jnp.where(quarter == k, picked[8 * k:8 * k + 8, 128 * q:128 * q + 128], tile)
        fold[q] = tile
    out3 = []
    for d in range(1, NZ):
        copy = pltpu.make_async_remote_copy(
            src_ref=fold.at[(plane + d) % NG], dst_ref=r3.at[d - 1], send_sem=send3.at[d - 1],
            recv_sem=recv3.at[d - 1], device_id=z_device(d), device_id_type=MESH)
        copy.start()
        out3.append(copy)
    for d in range(1, NZ):
        out3[d - 1].wait_recv()
    scale = 1.0 / math.sqrt(131072)
    tiles = []
    for d in range(NG):
        first = fold[plane % NG] if d == 0 else r3[d - 1]
        tiles.append((first + r3[d + NG - 1]) * scale)
    rows = []
    for k in range(4):
        halves = []
        for h in range(2):
            piece = None
            for j in range(4):
                moved = tiles[4 * h + j]
                if j != k:
                    moved = pltpu.roll(moved, (j - k) % 4 * 32, 1)
                piece = moved if piece is None else jnp.where(quarter == j, moved, piece)
            halves.append(piece)
        rows.append(jnp.concatenate(halves, axis=1))
    mine = NXY * core + xy
    g[mine] = jnp.concatenate(rows, axis=0).astype(jnp.bfloat16)

    out5 = []

    def forward(d, block):
        copy = pltpu.make_async_remote_copy(
            src_ref=g.at[block], dst_ref=g.at[block], send_sem=send5.at[d], recv_sem=recv5.at[d],
            device_id=sibling, device_id_type=MESH)
        copy.start()
        out5.append(copy)

    out4 = []
    for d in range(1, NXY):
        copy = pltpu.make_async_remote_copy(
            src_ref=g.at[mine], dst_ref=g.at[mine], send_sem=send4.at[d - 1], recv_sem=recv4.at[d - 1],
            device_id=xy_device(d), device_id_type=MESH)
        copy.start()
        out4.append(copy)
    forward(0, mine)
    for d in range(1, NXY):
        out4[d - 1].wait_recv()
        came = (px - d // NY + NX) % NX * NY + (py - d % NY + NY) % NY
        forward(d, NXY * core + came)
    for copy in out5:
        copy.wait_recv()

    own = g[f // 2, pl.ds(pl.multiple_of(f % 2 * 16, 16), 16), :]
    concept = lax.broadcasted_iota(jnp.int32, (16, 256), 1) % 32 // 8
    left = jnp.concatenate([jnp.where(concept == k, own, jnp.zeros_like(own)) for k in range(4)], axis=0)
    gram = lax.dot_general(left, g[...].reshape(1024, 256), (((1,), (1,)), ((), ())),
                           preferred_element_type=jnp.float32)
    out_ref[...] = (gram * (C / 1024)).reshape(4, 16, 1024)
    pair.wait_send()
    for copy in out2 + out3 + out4 + out5:
        copy.wait_send()


def body(features, signs, columns, labels):
    vmem = pl.BlockSpec(memory_space=pltpu.VMEM)
    dma = pltpu.SemaphoreType.DMA
    return pl.pallas_call(
        kernel,
        out_shape=jax.ShapeDtypeStruct((4, 16, 1024), jnp.float32),
        in_specs=[vmem] * 4,
        out_specs=vmem,
        scratch_shapes=[
            pltpu.VMEM((128, 2048), jnp.bfloat16),
            pltpu.VMEM((128, 2048), jnp.bfloat16),
            pltpu.VMEM((32, 32, 128), jnp.float32),
            pltpu.VMEM((16, 32, 128), jnp.float32),
            pltpu.VMEM((15, 32, 128), jnp.float32),
            pltpu.VMEM((8, 8, 128), jnp.float32),
            pltpu.VMEM((15, 8, 128), jnp.float32),
            pltpu.VMEM((32, 32, 256), jnp.bfloat16),
            dma, dma, dma((15,)), dma((15,)), dma((15,)), dma((15,)), dma((15,)), dma((15,)),
            dma((16,)), dma((16,)),
        ],
        compiler_params=pltpu.CompilerParams(
            collective_id=0, has_side_effects=True, vmem_limit_bytes=32 * 1024 * 1024),
    )(features, signs.reshape(1, -1), columns.reshape(8, 128), labels.reshape(1, 128))


def solution(mesh):
    in_specs = (P("tok", "feat"), P("feat"), P(), P("tok", None))
    out_specs = P("tok", "feat", None)
    return jax.shard_map(body, mesh=mesh, in_specs=in_specs, out_specs=out_specs, check_vma=False)
```

```python
import math

import jax
import jax.numpy as jnp
from jax import lax
from jax.experimental import pallas as pl
from jax.experimental.pallas import tpu as pltpu
from jax.sharding import PartitionSpec as P

C = 32
MESH = pl.DeviceIdType.MESH
NX, NH, NY, NC, NG = 4, 2, 4, 2, 8
NXY = NX * NY
NZ = NH * NG


FAR_XY = (10, 6, 14, 9, 11, 2, 8, 5, 7, 13, 15, 1, 3, 4, 12)
FAR_Z = (8, 7, 9, 6, 10, 5, 11, 4, 12, 3, 13, 2, 14, 1, 15)


def kernel(x_hbm, sg_hbm, col_hbm, lab_hbm, out_ref, x_ref, sg_ref, col_ref, lab_ref, xs, s, y, r1, r2, fold, r3, g,
           rows32, give, take, load, send1, recv1, send2, recv2, send3, recv3, send4, recv4, send5, recv5, send6, recv6):
    loads = [pltpu.make_async_copy(*pair, load.at[i]) for i, pair in enumerate(
        ((x_hbm, x_ref), (sg_hbm, sg_ref), (col_hbm, col_ref), (lab_hbm, lab_ref)))]
    for copy in loads:
        copy.start()
    f = lax.axis_index("feat")
    tok = lax.axis_index("tok")
    core = f % NC
    py = f // NC % NY
    zh = f // (NC * NY) % NH
    px = f // (NC * NY * NH)
    xy = px * NY + py
    plane = zh * NG + tok

    def feat_of(qx, qh, qy, qc):
        return ((qx * NH + qh) * NY + qy) * NC + qc

    sibling = {"feat": feat_of(px, zh, py, 1 - core), "tok": tok}

    def xy_at(d):
        return (px + d // NY) % NX, (py + d % NY) % NY

    def xy_device(d):
        qx, qy = xy_at(d)
        return {"feat": feat_of(qx, zh, qy, core), "tok": tok}

    def z_device(d):
        other = (plane + d) % NZ
        return {"feat": feat_of(px, other // NG, py, core), "tok": other % NG}

    barrier = pltpu.get_barrier_semaphore()
    for d in FAR_Z:
        pl.semaphore_signal(barrier, inc=1, device_id=z_device(d), device_id_type=MESH)
    for d in FAR_XY:
        pl.semaphore_signal(barrier, inc=1, device_id=xy_device(d), device_id_type=MESH)
    pl.semaphore_signal(barrier, inc=1, device_id=sibling, device_id_type=MESH)
    for copy in loads:
        copy.wait()

    xs[...] = x_ref[...] * sg_ref[...].astype(jnp.float32).astype(jnp.bfloat16)
    lane = lax.broadcasted_iota(jnp.int32, (128, 128), 1)

    def chunk(i):
        c = jnp.broadcast_to(col_ref[pl.ds(i, 1), :], (128, 128)).T
        v = (c & lane) ^ (c >> 11 & f)
        v = v ^ v >> 4
        v = v ^ v >> 2
        v = v ^ v >> 1
        parts = [(1 - 2 * (v & 1)).astype(jnp.float32).astype(jnp.bfloat16)]
        for bit in range(4):
            flip = (1 - 2 * (c >> 7 + bit & 1)).astype(jnp.float32).astype(jnp.bfloat16)
            parts = parts + [part * flip for part in parts]
        for block in range(16):
            s[:, 128 * block:128 * block + 128] = parts[block]
        found = lax.dot_general(s[...], xs[...], (((1,), (1,)), ((), ())), preferred_element_type=jnp.float32)
        y[pl.ds(4 * i, 4)] = found.reshape(4, 32, 128)

    @pl.loop(0, 4)
    def _(n):
        chunk(4 * (1 - core) + n)

    pl.semaphore_wait(barrier, 1 + (NXY - 1) + (NZ - 1))
    pair = pltpu.make_async_remote_copy(
        src_ref=y.at[pl.ds(NXY * (1 - core), NXY)], dst_ref=r1, send_sem=send1, recv_sem=recv1,
        device_id=sibling, device_id_type=MESH)
    pair.start()

    @pl.loop(0, 4)
    def _(n):
        chunk(4 * core + n)

    row = jnp.broadcast_to(lab_ref[...], (128, 128))
    col = row.T
    above = lax.broadcasted_iota(jnp.int32, (128, 128), 0)
    earlier = jnp.where((row == col) & (lane < above), 1.0, 0.0)
    rank = jnp.sum(earlier, axis=1, keepdims=True)
    slot = col.astype(jnp.float32) * 8.0 + rank
    within = (lane % 32).astype(jnp.float32)
    spread = jnp.concatenate(
        [jnp.where(slot == within + 32.0 * q, 1.0, 0.0).astype(jnp.bfloat16) for q in range(NG)], axis=1)

    pair.wait_recv()
    out2 = []
    for d in FAR_XY:
        qx, qy = xy_at(d)
        there = qx * NY + qy
        mine = NXY * core + there
        y[mine] = y[mine] + r1[there]
        copy = pltpu.make_async_remote_copy(
            src_ref=y.at[mine], dst_ref=r2.at[d - 1], send_sem=send2.at[d - 1], recv_sem=recv2.at[d - 1],
            device_id=xy_device(d), device_id_type=MESH)
        copy.start()
        out2.append(copy)
    total = y[NXY * core + xy] + r1[xy]
    for copy, d in zip(out2, FAR_XY):
        copy.wait_recv()
    for d in range(1, NXY):
        total = total + r2[d - 1]

    hi = total.astype(jnp.bfloat16)
    rest = total - hi.astype(jnp.float32)
    mid = rest.astype(jnp.bfloat16)
    low = (rest - mid.astype(jnp.float32)).astype(jnp.bfloat16)
    picked = jnp.dot(jnp.concatenate([hi, mid, low], axis=0), spread, preferred_element_type=jnp.float32)
    picked = picked[0:32] + picked[32:64] + picked[64:96]
    quarter = lax.broadcasted_iota(jnp.int32, (8, 128), 1) // 32
    for q in range(NG):
        tile = picked[0:8, 128 * q:128 * q + 128]
        for k in range(1, 4):
            tile = jnp.where(quarter == k, picked[8 * k:8 * k + 8, 128 * q:128 * q + 128], tile)
        fold[q] = tile
    out3 = []
    for d in FAR_Z:
        copy = pltpu.make_async_remote_copy(
            src_ref=fold.at[(plane + d) % NG], dst_ref=r3.at[d - 1], send_sem=send3.at[d - 1],
            recv_sem=recv3.at[d - 1], device_id=z_device(d), device_id_type=MESH)
        copy.start()
        out3.append(copy)
    for copy in out3:
        copy.wait_recv()
    scale = 1.0 / math.sqrt(131072)
    tiles = []
    for d in range(NG):
        first = fold[plane % NG] if d == 0 else r3[d - 1]
        tiles.append((first + r3[d + NG - 1]) * scale)
    rows = []
    for k in range(4):
        halves = []
        for h in range(2):
            piece = None
            for j in range(4):
                moved = tiles[4 * h + j]
                if j != k:
                    moved = pltpu.roll(moved, (j - k) % 4 * 32, 1)
                piece = moved if piece is None else jnp.where(quarter == j, moved, piece)
            halves.append(piece)
        rows.append(jnp.concatenate(halves, axis=1))
    g[xy] = jnp.concatenate(rows, axis=0).astype(jnp.bfloat16)

    out4 = {}
    for d in FAR_XY:
        out4[d] = pltpu.make_async_remote_copy(
            src_ref=g.at[xy], dst_ref=g.at[xy], send_sem=send4.at[d - 1], recv_sem=recv4.at[d - 1],
            device_id=xy_device(d), device_id_type=MESH)
        out4[d].start()

    wanted = 8 * px + 4 * zh + py
    holder = wanted // NXY == core
    where = wanted % NXY
    hand = pltpu.make_async_remote_copy(
        src_ref=g.at[where], dst_ref=rows32, send_sem=send5, recv_sem=recv5,
        device_id=sibling, device_id_type=MESH)
    shift = (px - where // NY + NX) % NX

    @pl.when(holder & (shift == 0))
    def _():
        hand.start()

    for step in (1, 3, 2):
        out4[NY * step].wait_recv()

        @pl.when(holder & (shift == step))
        def _():
            hand.start()

    for d in FAR_XY[::-1]:
        if d % NY:
            out4[d].wait_recv()

    @pl.when(holder)
    def _():
        hand.wait_send()
        rows32[...] = g[where]

    @pl.when(jnp.logical_not(holder))
    def _():
        hand.wait_recv()

    concept = lax.broadcasted_iota(jnp.int32, (16, 256), 1) % 32 // 8
    half = g[...].reshape(512, 256)

    def gram(part):
        own = rows32[pl.ds(pl.multiple_of(16 * part, 16), 16), :]
        left = jnp.concatenate([jnp.where(concept == k, own, jnp.zeros_like(own)) for k in range(4)], axis=0)
        found = lax.dot_general(left, half, (((1,), (1,)), ((), ())), preferred_element_type=jnp.float32)
        return found * (C / 1024)

    give[...] = gram(1 - core)
    swap = pltpu.make_async_remote_copy(
        src_ref=give, dst_ref=take, send_sem=send6, recv_sem=recv6, device_id=sibling, device_id_type=MESH)
    swap.start()
    out_ref[:, :, pl.ds(pl.multiple_of(512 * core, 512), 512)] = gram(core).reshape(4, 16, 512)
    for copy in [pair] + out2 + out3 + list(out4.values()):
        copy.wait_send()
    swap.wait_recv()
    out_ref[:, :, pl.ds(pl.multiple_of(512 * (1 - core), 512), 512)] = take[...].reshape(4, 16, 512)
    swap.wait_send()


def body(features, signs, columns, labels):
    vmem = pl.BlockSpec(memory_space=pltpu.VMEM)
    dma = pltpu.SemaphoreType.DMA
    return pl.pallas_call(
        kernel,
        out_shape=jax.ShapeDtypeStruct((4, 16, 1024), jnp.float32),
        in_specs=[pl.BlockSpec(memory_space=pltpu.HBM)] * 4,
        out_specs=vmem,
        scratch_shapes=[
            pltpu.VMEM((128, 2048), jnp.bfloat16),
            pltpu.VMEM((1, 2048), jnp.int32),
            pltpu.VMEM((8, 128), jnp.int32),
            pltpu.VMEM((1, 128), jnp.int32),
            pltpu.VMEM((128, 2048), jnp.bfloat16),
            pltpu.VMEM((128, 2048), jnp.bfloat16),
            pltpu.VMEM((32, 32, 128), jnp.float32),
            pltpu.VMEM((16, 32, 128), jnp.float32),
            pltpu.VMEM((15, 32, 128), jnp.float32),
            pltpu.VMEM((8, 8, 128), jnp.float32),
            pltpu.VMEM((15, 8, 128), jnp.float32),
            pltpu.VMEM((16, 32, 256), jnp.bfloat16),
            pltpu.VMEM((32, 256), jnp.bfloat16),
            pltpu.VMEM((64, 512), jnp.float32),
            pltpu.VMEM((64, 512), jnp.float32),
            dma((4,)), dma, dma, dma((15,)), dma((15,)), dma((15,)), dma((15,)), dma((15,)), dma((15,)),
            dma, dma, dma, dma,
        ],
        compiler_params=pltpu.CompilerParams(
            collective_id=0, has_side_effects=True, vmem_limit_bytes=54784 * 1024),
    )(features, signs.reshape(1, -1), columns.reshape(8, 128), labels.reshape(1, 128))


def solution(mesh):
    in_specs = (P("tok", "feat"), P("feat"), P(), P("tok", None))
    out_specs = P("tok", "feat", None)
    return jax.shard_map(body, mesh=mesh, in_specs=in_specs, out_specs=out_specs, check_vma=False)
```

```python
import math

import jax
import jax.numpy as jnp
from jax import lax
from jax.experimental import pallas as pl
from jax.experimental.pallas import tpu as pltpu
from jax.sharding import PartitionSpec as P

C = 32
MESH = pl.DeviceIdType.MESH
NX, NH, NY, NC, NG = 4, 2, 4, 2, 8
NXY = NX * NY
NZ = NH * NG


FAR_XY = (10, 6, 14, 9, 11, 2, 8, 5, 7, 13, 15, 1, 3, 4, 12)
FAR_Z = (8, 7, 9, 6, 10, 5, 11, 4, 12, 3, 13, 2, 14, 1, 15)


def kernel(x_hbm, sg_hbm, col_hbm, lab_hbm, out_ref, x_ref, sg_ref, col_ref, lab_ref, xs, s, flip, y, r1, r2, fold, r3, g,
           rows32, give, take, load, send1, recv1, send2, recv2, send3, recv3, send4, recv4, send5, recv5, send6, recv6,
           plane_here, line_here):
    loads = [pltpu.make_async_copy(*pair, load.at[i]) for i, pair in enumerate(
        ((x_hbm, x_ref), (sg_hbm, sg_ref), (col_hbm, col_ref), (lab_hbm, lab_ref)))]
    for copy in loads:
        copy.start()
    f = lax.axis_index("feat")
    tok = lax.axis_index("tok")
    core = f % NC
    py = f // NC % NY
    zh = f // (NC * NY) % NH
    px = f // (NC * NY * NH)
    xy = px * NY + py
    plane = zh * NG + tok

    def feat_of(qx, qh, qy, qc):
        return ((qx * NH + qh) * NY + qy) * NC + qc

    sibling = {"feat": feat_of(px, zh, py, 1 - core), "tok": tok}

    def xy_at(d):
        return (px + d // NY) % NX, (py + d % NY) % NY

    def xy_device(d, c):
        qx, qy = xy_at(d)
        return {"feat": feat_of(qx, zh, qy, c), "tok": tok}

    def z_device(d, c):
        other = (plane + d) % NZ
        return {"feat": feat_of(px, other // NG, py, c), "tok": other % NG}

    def signal(sem, device):
        pl.semaphore_signal(sem, inc=1, device_id=device, device_id_type=MESH)

    barrier = pltpu.get_barrier_semaphore()
    for d in FAR_XY:
        signal(barrier, xy_device(d, 0))

    @pl.when(core == 1)
    def _():
        signal(barrier, sibling)

    for d in FAR_Z:
        signal(barrier, z_device(d, 1))

    loads[2].wait()
    lane = lax.broadcasted_iota(jnp.int32, (128, 128), 1)

    @pl.loop(0, 8)
    def _(i):
        c = jnp.broadcast_to(col_ref[pl.ds(i, 1), :], (128, 128)).T
        v = (c & lane) ^ (c >> 11 & f)
        v = v ^ v >> 4
        v = v ^ v >> 2
        v = v ^ v >> 1
        parts = [(1 - 2 * (v & 1)).astype(jnp.float32).astype(jnp.bfloat16)]
        for bit in range(3):
            turn = (1 - 2 * (c >> 7 + bit & 1)).astype(jnp.float32).astype(jnp.bfloat16)
            parts = parts + [part * turn for part in parts]
        for block in range(8):
            s[i, :, 128 * block:128 * block + 128] = parts[block]
        flip[i] = (1 - 2 * (c >> 10 & 1)).astype(jnp.float32)

    for i in (0, 1, 3):
        loads[i].wait()
    sign = sg_ref[...].astype(jnp.float32).astype(jnp.bfloat16)
    for h in range(2):
        xs[128 * h:128 * h + 128, :] = x_ref[:, 1024 * h:1024 * h + 1024] * sign[:, 1024 * h:1024 * h + 1024]

    def half_of(c):
        kept = s[pl.ds(4 * c, 4)].reshape(512, 1024)
        found = lax.dot_general(kept, xs[...], (((1,), (1,)), ((), ())), preferred_element_type=jnp.float32)
        found = found[:, :128] + found[:, 128:] * flip[pl.ds(4 * c, 4)].reshape(512, 128)
        y[pl.ds(NXY * c, NXY)] = found.reshape(NXY, 32, 128)

    half_of(1 - core)

    @pl.when(core == 0)
    def _():
        pl.semaphore_wait(barrier, 2 * (NXY - 1) + 1)
        signal(plane_here, sibling)

    @pl.when(core == 1)
    def _():
        pl.semaphore_wait(plane_here, 1)

    pair = pltpu.make_async_remote_copy(
        src_ref=y.at[pl.ds(NXY * (1 - core), NXY)], dst_ref=r1, send_sem=send1, recv_sem=recv1,
        device_id=sibling, device_id_type=MESH)
    pair.start()
    half_of(core)

    row = jnp.broadcast_to(lab_ref[...], (128, 128))
    col = row.T
    above = lax.broadcasted_iota(jnp.int32, (128, 128), 0)
    earlier = jnp.where((row == col) & (lane < above), 1.0, 0.0)
    rank = jnp.sum(earlier, axis=1, keepdims=True)
    slot = col.astype(jnp.float32) * 8.0 + rank
    within = (lane % 32).astype(jnp.float32)
    spread = jnp.concatenate(
        [jnp.where(slot == within + 32.0 * q, 1.0, 0.0).astype(jnp.bfloat16) for q in range(NG)], axis=1)

    pair.wait_recv()
    out2 = []
    for d in FAR_XY:
        qx, qy = xy_at(d)
        there = qx * NY + qy
        mine = NXY * core + there
        y[mine] = y[mine] + r1[there]
        copy = pltpu.make_async_remote_copy(
            src_ref=y.at[mine], dst_ref=r2.at[d - 1], send_sem=send2.at[d - 1], recv_sem=recv2.at[d - 1],
            device_id=xy_device(d, core), device_id_type=MESH)
        copy.start()
        out2.append(copy)
    total = y[NXY * core + xy] + r1[xy]

    @pl.when(core == 1)
    def _():
        pl.semaphore_wait(barrier, 2 * (NZ - 1))
        signal(line_here, sibling)

    @pl.when(core == 0)
    def _():
        pl.semaphore_wait(line_here, 1)

    for copy, d in zip(out2, FAR_XY):
        copy.wait_recv()
    for d in range(1, NXY):
        total = total + r2[d - 1]

    hi = total.astype(jnp.bfloat16)
    rest = total - hi.astype(jnp.float32)
    mid = rest.astype(jnp.bfloat16)
    low = (rest - mid.astype(jnp.float32)).astype(jnp.bfloat16)
    picked = jnp.dot(jnp.concatenate([hi, mid, low], axis=0), spread, preferred_element_type=jnp.float32)
    picked = picked[0:32] + picked[32:64] + picked[64:96]
    quarter = lax.broadcasted_iota(jnp.int32, (8, 128), 1) // 32
    for q in range(NG):
        tile = picked[0:8, 128 * q:128 * q + 128]
        for k in range(1, 4):
            tile = jnp.where(quarter == k, picked[8 * k:8 * k + 8, 128 * q:128 * q + 128], tile)
        fold[q] = tile
    out3 = []
    for d in FAR_Z:
        copy = pltpu.make_async_remote_copy(
            src_ref=fold.at[(plane + d) % NG], dst_ref=r3.at[d - 1], send_sem=send3.at[d - 1],
            recv_sem=recv3.at[d - 1], device_id=z_device(d, core), device_id_type=MESH)
        copy.start()
        out3.append(copy)
    for copy in out3:
        copy.wait_recv()
    scale = 1.0 / math.sqrt(131072)
    tiles = []
    for d in range(NG):
        first = fold[plane % NG] if d == 0 else r3[d - 1]
        tiles.append((first + r3[d + NG - 1]) * scale)
    rows = []
    for k in range(4):
        halves = []
        for h in range(2):
            piece = None
            for j in range(4):
                moved = tiles[4 * h + j]
                if j != k:
                    moved = pltpu.roll(moved, (j - k) % 4 * 32, 1)
                piece = moved if piece is None else jnp.where(quarter == j, moved, piece)
            halves.append(piece)
        rows.append(jnp.concatenate(halves, axis=1))
    g[xy] = jnp.concatenate(rows, axis=0).astype(jnp.bfloat16)

    out4 = {}
    for d in FAR_XY:
        out4[d] = pltpu.make_async_remote_copy(
            src_ref=g.at[xy], dst_ref=g.at[xy], send_sem=send4.at[d - 1], recv_sem=recv4.at[d - 1],
            device_id=xy_device(d, core), device_id_type=MESH)
        out4[d].start()

    wanted = 8 * px + 4 * zh + py
    holder = wanted // NXY == core
    where = wanted % NXY
    hand = pltpu.make_async_remote_copy(
        src_ref=g.at[where], dst_ref=rows32, send_sem=send5, recv_sem=recv5,
        device_id=sibling, device_id_type=MESH)
    shift = (px - where // NY + NX) % NX

    @pl.when(holder & (shift == 0))
    def _():
        hand.start()

    for step in (1, 3, 2):
        out4[NY * step].wait_recv()

        @pl.when(holder & (shift == step))
        def _():
            hand.start()

    @pl.when(holder)
    def _():
        hand.wait_send()
        rows32[...] = g[where]

    @pl.when(jnp.logical_not(holder))
    def _():
        hand.wait_recv()

    concept = lax.broadcasted_iota(jnp.int32, (16, 256), 1) % 32 // 8

    def left_of(part):
        own = rows32[pl.ds(pl.multiple_of(16 * part, 16), 16), :]
        return [jnp.where(concept == k, own, jnp.zeros_like(own)) for k in range(4)]

    left = jnp.concatenate(left_of(1 - core) + left_of(core), axis=0)
    swaps = []
    for step in (0, 1, 3, 2):
        for dy in (1, 3, 2):
            out4[NY * step + dy].wait_recv()
        came = (px - step + NX) % NX
        quarter_rows = g[pl.ds(4 * came, 4)].reshape(128, 256)
        found = lax.dot_general(left, quarter_rows, (((1,), (1,)), ((), ())), preferred_element_type=jnp.float32)
        found = found * (C / 1024)
        give[step] = found[:64]
        swap = pltpu.make_async_remote_copy(
            src_ref=give.at[step], dst_ref=take.at[step], send_sem=send6.at[step], recv_sem=recv6.at[step],
            device_id=sibling, device_id_type=MESH)
        swap.start()
        swaps.append((swap, step, came))
        at = pl.multiple_of(512 * core + 128 * came, 128)
        out_ref[:, :, pl.ds(at, 128)] = found[64:].reshape(4, 16, 128)
    for copy in [pair] + out2 + out3 + list(out4.values()):
        copy.wait_send()
    for swap, step, came in swaps:
        swap.wait_recv()
        at = pl.multiple_of(512 * (1 - core) + 128 * came, 128)
        out_ref[:, :, pl.ds(at, 128)] = take[step].reshape(4, 16, 128)
    for swap, step, came in swaps:
        swap.wait_send()


def body(features, signs, columns, labels):
    vmem = pl.BlockSpec(memory_space=pltpu.VMEM)
    dma = pltpu.SemaphoreType.DMA
    return pl.pallas_call(
        kernel,
        out_shape=jax.ShapeDtypeStruct((4, 16, 1024), jnp.float32),
        in_specs=[pl.BlockSpec(memory_space=pltpu.HBM)] * 4,
        out_specs=vmem,
        scratch_shapes=[
            pltpu.VMEM((128, 2048), jnp.bfloat16),
            pltpu.VMEM((1, 2048), jnp.int32),
            pltpu.VMEM((8, 128), jnp.int32),
            pltpu.VMEM((1, 128), jnp.int32),
            pltpu.VMEM((256, 1024), jnp.bfloat16),
            pltpu.VMEM((8, 128, 1024), jnp.bfloat16),
            pltpu.VMEM((8, 128, 128), jnp.float32),
            pltpu.VMEM((32, 32, 128), jnp.float32),
            pltpu.VMEM((16, 32, 128), jnp.float32),
            pltpu.VMEM((15, 32, 128), jnp.float32),
            pltpu.VMEM((8, 8, 128), jnp.float32),
            pltpu.VMEM((15, 8, 128), jnp.float32),
            pltpu.VMEM((16, 32, 256), jnp.bfloat16),
            pltpu.VMEM((32, 256), jnp.bfloat16),
            pltpu.VMEM((4, 64, 128), jnp.float32),
            pltpu.VMEM((4, 64, 128), jnp.float32),
            dma((4,)), dma, dma, dma((15,)), dma((15,)), dma((15,)), dma((15,)), dma((15,)), dma((15,)),
            dma, dma, dma((4,)), dma((4,)), pltpu.SemaphoreType.REGULAR, pltpu.SemaphoreType.REGULAR,
        ],
        compiler_params=pltpu.CompilerParams(
            collective_id=0, has_side_effects=True, vmem_limit_bytes=54784 * 1024),
    )(features, signs.reshape(1, -1), columns.reshape(8, 128), labels.reshape(1, 128))


def solution(mesh):
    in_specs = (P("tok", "feat"), P("feat"), P(), P("tok", None))
    out_specs = P("tok", "feat", None)
    return jax.shard_map(body, mesh=mesh, in_specs=in_specs, out_specs=out_specs, check_vma=False)
```

```python
import math

import jax
import jax.numpy as jnp
from jax import lax
from jax.experimental import pallas as pl
from jax.experimental.pallas import tpu as pltpu
from jax.sharding import PartitionSpec as P

C = 32
MESH = pl.DeviceIdType.MESH
NX, NH, NY, NC, NG = 4, 2, 4, 2, 8
NXY = NX * NY
NZ = NH * NG


FAR_XY = (10, 6, 14, 9, 11, 2, 8, 5, 7, 13, 15, 1, 3, 4, 12)
FAR_Z = (8, 7, 9, 6, 10, 5, 11, 4, 12, 3, 13, 2, 14, 1, 15)


def kernel(x_hbm, sg_hbm, col_hbm, lab_hbm, out_ref, x_ref, sg_ref, col_ref, lab_ref, xs, s, flip, y, r1, r2, fold, r3, g,
           rows32, give, take, load, send1, recv1, send2, recv2, send3, recv3, send4, recv4, send5, recv5, send6, recv6,
           plane_here, line_here):
    loads = [pltpu.make_async_copy(*pair, load.at[i]) for i, pair in enumerate(
        [(col_hbm, col_ref), (sg_hbm, sg_ref), (lab_hbm, lab_ref)]
        + [(x_hbm.at[pl.ds(16 * k, 16)], x_ref.at[pl.ds(16 * k, 16)]) for k in range(8)])]
    for copy in loads:
        copy.start()
    f = lax.axis_index("feat")
    tok = lax.axis_index("tok")
    core = f % NC
    py = f // NC % NY
    zh = f // (NC * NY) % NH
    px = f // (NC * NY * NH)
    xy = px * NY + py
    plane = zh * NG + tok

    def feat_of(qx, qh, qy, qc):
        return ((qx * NH + qh) * NY + qy) * NC + qc

    sibling = {"feat": feat_of(px, zh, py, 1 - core), "tok": tok}

    def xy_at(d):
        return (px + d // NY) % NX, (py + d % NY) % NY

    def xy_device(d, c):
        qx, qy = xy_at(d)
        return {"feat": feat_of(qx, zh, qy, c), "tok": tok}

    def z_device(d, c):
        other = (plane + d) % NZ
        return {"feat": feat_of(px, other // NG, py, c), "tok": other % NG}

    def signal(sem, device):
        pl.semaphore_signal(sem, inc=1, device_id=device, device_id_type=MESH)

    barrier = pltpu.get_barrier_semaphore()
    for d in FAR_XY:
        signal(barrier, xy_device(d, 0))

    @pl.when(core == 1)
    def _():
        signal(barrier, sibling)

    for d in FAR_Z:
        signal(barrier, z_device(d, 1))

    loads[0].wait()
    lane = lax.broadcasted_iota(jnp.int32, (128, 128), 1)

    @pl.loop(0, 8)
    def _(i):
        c = jnp.broadcast_to(col_ref[pl.ds(i, 1), :], (128, 128)).T
        v = (c & lane) ^ (c >> 11 & f)
        v = v ^ v >> 4
        v = v ^ v >> 2
        v = v ^ v >> 1
        parts = [(1 - 2 * (v & 1)).astype(jnp.float32).astype(jnp.bfloat16)]
        for bit in range(3):
            turn = (1 - 2 * (c >> 7 + bit & 1)).astype(jnp.float32).astype(jnp.bfloat16)
            parts = parts + [part * turn for part in parts]
        for block in range(8):
            s[i, :, 128 * block:128 * block + 128] = parts[block]
        flip[i] = (1 - 2 * (c >> 10 & 1)).astype(jnp.float32)

    for copy in loads[1:]:
        copy.wait()
    sign = sg_ref[...].astype(jnp.float32).astype(jnp.bfloat16)
    for h in range(2):
        xs[128 * h:128 * h + 128, :] = x_ref[:, 1024 * h:1024 * h + 1024] * sign[:, 1024 * h:1024 * h + 1024]

    def half_of(c):
        kept = s[pl.ds(4 * c, 4)].reshape(512, 1024)
        found = lax.dot_general(kept, xs[...], (((1,), (1,)), ((), ())), preferred_element_type=jnp.float32)
        found = found[:, :128] + found[:, 128:] * flip[pl.ds(4 * c, 4)].reshape(512, 128)
        y[pl.ds(NXY * c, NXY)] = found.reshape(NXY, 32, 128)

    half_of(1 - core)

    @pl.when(core == 0)
    def _():
        pl.semaphore_wait(barrier, 2 * (NXY - 1) + 1)
        signal(plane_here, sibling)

    @pl.when(core == 1)
    def _():
        pl.semaphore_wait(plane_here, 1)

    pair = pltpu.make_async_remote_copy(
        src_ref=y.at[pl.ds(NXY * (1 - core), NXY)], dst_ref=r1, send_sem=send1, recv_sem=recv1,
        device_id=sibling, device_id_type=MESH)
    pair.start()
    half_of(core)

    row = jnp.broadcast_to(lab_ref[...], (128, 128))
    col = row.T
    above = lax.broadcasted_iota(jnp.int32, (128, 128), 0)
    earlier = jnp.where((row == col) & (lane < above), 1.0, 0.0)
    rank = jnp.sum(earlier, axis=1, keepdims=True)
    slot = col.astype(jnp.float32) * 8.0 + rank
    within = (lane % 32).astype(jnp.float32)
    spread = jnp.concatenate(
        [jnp.where(slot == within + 32.0 * q, 1.0, 0.0).astype(jnp.bfloat16) for q in range(NG)], axis=1)

    pair.wait_recv()
    out2 = []
    for d in FAR_XY:
        qx, qy = xy_at(d)
        there = qx * NY + qy
        mine = NXY * core + there
        y[mine] = y[mine] + r1[there]
        copy = pltpu.make_async_remote_copy(
            src_ref=y.at[mine], dst_ref=r2.at[d - 1], send_sem=send2.at[d - 1], recv_sem=recv2.at[d - 1],
            device_id=xy_device(d, core), device_id_type=MESH)
        copy.start()
        out2.append(copy)
    total = y[NXY * core + xy] + r1[xy]

    @pl.when(core == 1)
    def _():
        pl.semaphore_wait(barrier, 2 * (NZ - 1))
        signal(line_here, sibling)

    @pl.when(core == 0)
    def _():
        pl.semaphore_wait(line_here, 1)

    for copy, d in zip(out2, FAR_XY):
        copy.wait_recv()
    for d in range(1, NXY):
        total = total + r2[d - 1]

    hi = total.astype(jnp.bfloat16)
    rest = total - hi.astype(jnp.float32)
    mid = rest.astype(jnp.bfloat16)
    low = (rest - mid.astype(jnp.float32)).astype(jnp.bfloat16)
    picked = jnp.dot(jnp.concatenate([hi, mid, low], axis=0), spread, preferred_element_type=jnp.float32)
    picked = picked[0:32] + picked[32:64] + picked[64:96]
    quarter = lax.broadcasted_iota(jnp.int32, (8, 128), 1) // 32
    for q in range(NG):
        tile = picked[0:8, 128 * q:128 * q + 128]
        for k in range(1, 4):
            tile = jnp.where(quarter == k, picked[8 * k:8 * k + 8, 128 * q:128 * q + 128], tile)
        fold[q] = tile
    out3 = []
    for d in FAR_Z:
        copy = pltpu.make_async_remote_copy(
            src_ref=fold.at[(plane + d) % NG], dst_ref=r3.at[d - 1], send_sem=send3.at[d - 1],
            recv_sem=recv3.at[d - 1], device_id=z_device(d, core), device_id_type=MESH)
        copy.start()
        out3.append(copy)
    for copy in out3:
        copy.wait_recv()
    scale = 1.0 / math.sqrt(131072)
    tiles = []
    for d in range(NG):
        first = fold[plane % NG] if d == 0 else r3[d - 1]
        tiles.append((first + r3[d + NG - 1]) * scale)
    rows = []
    for k in range(4):
        halves = []
        for h in range(2):
            piece = None
            for j in range(4):
                moved = tiles[4 * h + j]
                if j != k:
                    moved = pltpu.roll(moved, (j - k) % 4 * 32, 1)
                piece = moved if piece is None else jnp.where(quarter == j, moved, piece)
            halves.append(piece)
        rows.append(jnp.concatenate(halves, axis=1))
    g[xy] = jnp.concatenate(rows, axis=0).astype(jnp.bfloat16)

    out4 = {}
    for d in FAR_XY:
        out4[d] = pltpu.make_async_remote_copy(
            src_ref=g.at[xy], dst_ref=g.at[xy], send_sem=send4.at[d - 1], recv_sem=recv4.at[d - 1],
            device_id=xy_device(d, core), device_id_type=MESH)
        out4[d].start()

    wanted = 8 * px + 4 * zh + py
    holder = wanted // NXY == core
    where = wanted % NXY
    hand = pltpu.make_async_remote_copy(
        src_ref=g.at[where], dst_ref=rows32, send_sem=send5, recv_sem=recv5,
        device_id=sibling, device_id_type=MESH)
    shift = (px - where // NY + NX) % NX

    @pl.when(holder & (shift == 0))
    def _():
        hand.start()

    for step in (1, 3, 2):
        out4[NY * step].wait_recv()

        @pl.when(holder & (shift == step))
        def _():
            hand.start()

    @pl.when(holder)
    def _():
        hand.wait_send()
        rows32[...] = g[where]

    @pl.when(jnp.logical_not(holder))
    def _():
        hand.wait_recv()

    concept = lax.broadcasted_iota(jnp.int32, (16, 256), 1) % 32 // 8

    def left_of(part):
        own = rows32[pl.ds(pl.multiple_of(16 * part, 16), 16), :]
        return [jnp.where(concept == k, own, jnp.zeros_like(own)) for k in range(4)]

    left = jnp.concatenate(left_of(1 - core) + left_of(core), axis=0)
    swaps = []
    for step in (0, 1, 3, 2):
        for dy in (1, 3, 2):
            out4[NY * step + dy].wait_recv()
        came = (px - step + NX) % NX
        quarter_rows = g[pl.ds(4 * came, 4)].reshape(128, 256)
        found = lax.dot_general(left, quarter_rows, (((1,), (1,)), ((), ())), preferred_element_type=jnp.float32)
        found = found * (C / 1024)
        give[step] = found[:64]
        swap = pltpu.make_async_remote_copy(
            src_ref=give.at[step], dst_ref=take.at[step], send_sem=send6.at[step], recv_sem=recv6.at[step],
            device_id=sibling, device_id_type=MESH)
        swap.start()
        swaps.append((swap, step, came))
        at = pl.multiple_of(512 * core + 128 * came, 128)
        out_ref[:, :, pl.ds(at, 128)] = found[64:].reshape(4, 16, 128)
    for copy in [pair] + out2 + out3 + list(out4.values()):
        copy.wait_send()
    for swap, step, came in swaps:
        swap.wait_recv()
        at = pl.multiple_of(512 * (1 - core) + 128 * came, 128)
        out_ref[:, :, pl.ds(at, 128)] = take[step].reshape(4, 16, 128)
    for swap, step, came in swaps:
        swap.wait_send()


def body(features, signs, columns, labels):
    args = features, signs.reshape(1, -1), columns.reshape(8, 128), labels.reshape(1, 128)
    vmem = pl.BlockSpec(memory_space=pltpu.VMEM)
    dma = pltpu.SemaphoreType.DMA
    return pl.pallas_call(
        kernel,
        out_shape=jax.ShapeDtypeStruct((4, 16, 1024), jnp.float32),
        in_specs=[pl.BlockSpec(memory_space=pltpu.HBM)] * 4,
        out_specs=vmem,
        scratch_shapes=[
            pltpu.VMEM((128, 2048), jnp.bfloat16),
            pltpu.VMEM((1, 2048), jnp.int32),
            pltpu.VMEM((8, 128), jnp.int32),
            pltpu.VMEM((1, 128), jnp.int32),
            pltpu.VMEM((256, 1024), jnp.bfloat16),
            pltpu.VMEM((8, 128, 1024), jnp.bfloat16),
            pltpu.VMEM((8, 128, 128), jnp.float32),
            pltpu.VMEM((32, 32, 128), jnp.float32),
            pltpu.VMEM((16, 32, 128), jnp.float32),
            pltpu.VMEM((15, 32, 128), jnp.float32),
            pltpu.VMEM((8, 8, 128), jnp.float32),
            pltpu.VMEM((15, 8, 128), jnp.float32),
            pltpu.VMEM((16, 32, 256), jnp.bfloat16),
            pltpu.VMEM((32, 256), jnp.bfloat16),
            pltpu.VMEM((4, 64, 128), jnp.float32),
            pltpu.VMEM((4, 64, 128), jnp.float32),
            dma((11,)), dma, dma, dma((15,)), dma((15,)), dma((15,)), dma((15,)), dma((15,)), dma((15,)),
            dma, dma, dma((4,)), dma((4,)), pltpu.SemaphoreType.REGULAR, pltpu.SemaphoreType.REGULAR,
        ],
        compiler_params=pltpu.CompilerParams(
            collective_id=0, has_side_effects=True, vmem_limit_bytes=40 * 1024 * 1024),
    )(*[pltpu.with_memory_space_constraint(arg, pltpu.HBM) for arg in args])


def solution(mesh):
    in_specs = (P("tok", "feat"), P("feat"), P(), P("tok", None))
    out_specs = P("tok", "feat", None)
    return jax.shard_map(body, mesh=mesh, in_specs=in_specs, out_specs=out_specs, check_vma=False)
```

```python
import math

import jax
import jax.numpy as jnp
from jax import lax
from jax.experimental import pallas as pl
from jax.experimental.pallas import tpu as pltpu
from jax.sharding import PartitionSpec as P

C = 32
MESH = pl.DeviceIdType.MESH
NX, NH, NY, NC, NG = 4, 2, 4, 2, 8
NXY = NX * NY
NZ = NH * NG


FAR_XY = (10, 6, 14, 9, 11, 2, 8, 5, 7, 13, 15, 1, 3, 4, 12)
STEPS = (2, 1, 3, 0)
FAR_Z = (8, 7, 9, 6, 10, 5, 11, 4, 12, 3, 13, 2, 14, 1, 15)


def kernel(x_hbm, sg_hbm, col_hbm, lab_hbm, out_ref, x_ref, sg_ref, col_ref, lab_ref, xs, s, flip, y, r1, r2, fold, r3, g,
           rows32, give, take, load, send1, recv1, send2, recv2, send3, recv3, send4, recv4, send5, recv5, send6, recv6,
           both_here, all_here):
    loads = [pltpu.make_async_copy(*pair, load.at[i]) for i, pair in enumerate(
        [(col_hbm, col_ref), (sg_hbm, sg_ref), (lab_hbm, lab_ref)]
        + [(x_hbm.at[pl.ds(16 * k, 16)], x_ref.at[pl.ds(16 * k, 16)]) for k in range(8)])]
    for copy in loads:
        copy.start()
    f = lax.axis_index("feat")
    tok = lax.axis_index("tok")
    core = f % NC
    py = f // NC % NY
    zh = f // (NC * NY) % NH
    px = f // (NC * NY * NH)
    xy = px * NY + py
    plane = zh * NG + tok

    def feat_of(qx, qh, qy, qc):
        return ((qx * NH + qh) * NY + qy) * NC + qc

    sibling = {"feat": feat_of(px, zh, py, 1 - core), "tok": tok}

    def xy_at(d):
        return (px + d // NY) % NX, (py + d % NY) % NY

    def xy_device(d, c):
        qx, qy = xy_at(d)
        return {"feat": feat_of(qx, zh, qy, c), "tok": tok}

    def z_device(d, c):
        other = (plane + d) % NZ
        return {"feat": feat_of(px, other // NG, py, c), "tok": other % NG}

    def signal(sem, device):
        pl.semaphore_signal(sem, inc=1, device_id=device, device_id_type=MESH)

    barrier = pltpu.get_barrier_semaphore()

    @pl.when(core == 0)
    def _():
        signal(barrier, sibling)

    for d in FAR_Z:
        signal(barrier, z_device(d, 0))
    for d in FAR_XY:
        signal(barrier, xy_device(d, 0))

    @pl.when(core == 1)
    def _():
        pl.semaphore_wait(barrier, 1)
        signal(both_here, sibling)

    loads[0].wait()
    lane = lax.broadcasted_iota(jnp.int32, (128, 128), 1)
    kept_at = col_ref[...]
    high = kept_at >> 11 & f
    for shift in (4, 2, 1):
        high = high ^ high >> shift
    code = kept_at & 127 | (high & 1) << 7 | (kept_at & 1920) << 1
    for i in range(8):
        c = jnp.broadcast_to(code[i:i + 1, :], (128, 128)).T
        v = c & (lane | 128)
        for shift in (4, 2, 1):
            v = v ^ v >> shift
        parts = [(1 - 2 * (v & 1)).astype(jnp.float32).astype(jnp.bfloat16)]
        for bit in range(3):
            turn = (1 - 2 * (c >> 8 + bit & 1)).astype(jnp.float32).astype(jnp.bfloat16)
            parts = parts + [part * turn for part in parts]
        for block in range(8):
            s[i, :, 128 * block:128 * block + 128] = parts[block]
        flip[i] = (1 - 2 * (c >> 11 & 1)).astype(jnp.float32)

    for copy in loads[1:]:
        copy.wait()
    sign = sg_ref[...].astype(jnp.float32).astype(jnp.bfloat16)
    for h in range(2):
        xs[128 * h:128 * h + 128, :] = x_ref[:, 1024 * h:1024 * h + 1024] * sign[:, 1024 * h:1024 * h + 1024]

    def half_of(c):
        kept = s[pl.ds(4 * c, 4)].reshape(512, 1024)
        found = lax.dot_general(kept, xs[...], (((1,), (1,)), ((), ())), preferred_element_type=jnp.float32)
        found = found[:, :128] + found[:, 128:] * flip[pl.ds(4 * c, 4)].reshape(512, 128)
        y[pl.ds(NXY * c, NXY)] = found.reshape(NXY, 32, 128)

    half_of(1 - core)

    @pl.when(core == 0)
    def _():
        pl.semaphore_wait(both_here, 1)

    pairs = []
    for k, step in enumerate(STEPS):
        there = 4 * ((px + step) % NX)
        pairs.append(pltpu.make_async_remote_copy(
            src_ref=y.at[pl.ds(NXY * (1 - core) + there, 4)], dst_ref=r1.at[pl.ds(there, 4)],
            send_sem=send1.at[k], recv_sem=recv1.at[k], device_id=sibling, device_id_type=MESH))
        pairs[k].start()
    half_of(core)

    row = jnp.broadcast_to(lab_ref[...], (128, 128))
    col = row.T
    above = lax.broadcasted_iota(jnp.int32, (128, 128), 0)
    earlier = jnp.where((row == col) & (lane < above), 1.0, 0.0)
    rank = jnp.sum(earlier, axis=1, keepdims=True)
    slot = col.astype(jnp.float32) * 8.0 + rank
    within = (lane % 32).astype(jnp.float32)
    spread = jnp.concatenate(
        [jnp.where(slot == within + 32.0 * q, 1.0, 0.0).astype(jnp.bfloat16) for q in range(NG)], axis=1)

    @pl.when(core == 0)
    def _():
        pl.semaphore_wait(barrier, 2 * (NXY - 1) + 2 * (NZ - 1))
        signal(all_here, sibling)

    @pl.when(core == 1)
    def _():
        pl.semaphore_wait(all_here, 1)

    out2 = []
    for k, step in enumerate(STEPS):
        pairs[k].wait_recv()
        for d in [NY * step + dy for dy in (2, 1, 3, 0) if step or dy]:
            qx, qy = xy_at(d)
            there = qx * NY + qy
            mine = NXY * core + there
            y[mine] = y[mine] + r1[there]
            copy = pltpu.make_async_remote_copy(
                src_ref=y.at[mine], dst_ref=r2.at[d - 1], send_sem=send2.at[d - 1], recv_sem=recv2.at[d - 1],
                device_id=xy_device(d, core), device_id_type=MESH)
            copy.start()
            out2.append(copy)
    total = y[NXY * core + xy] + r1[xy]

    for copy in out2:
        copy.wait_recv()
    for d in range(1, NXY):
        total = total + r2[d - 1]

    hi = total.astype(jnp.bfloat16)
    rest = total - hi.astype(jnp.float32)
    mid = rest.astype(jnp.bfloat16)
    low = (rest - mid.astype(jnp.float32)).astype(jnp.bfloat16)
    picked = jnp.dot(jnp.concatenate([hi, mid, low], axis=0), spread, preferred_element_type=jnp.float32)
    picked = picked[0:32] + picked[32:64] + picked[64:96]
    quarter = lax.broadcasted_iota(jnp.int32, (8, 128), 1) // 32
    for q in range(NG):
        tile = picked[0:8, 128 * q:128 * q + 128]
        for k in range(1, 4):
            tile = jnp.where(quarter == k, picked[8 * k:8 * k + 8, 128 * q:128 * q + 128], tile)
        fold[q] = tile
    out3 = []
    for d in FAR_Z:
        copy = pltpu.make_async_remote_copy(
            src_ref=fold.at[(plane + d) % NG], dst_ref=r3.at[d - 1], send_sem=send3.at[d - 1],
            recv_sem=recv3.at[d - 1], device_id=z_device(d, core), device_id_type=MESH)
        copy.start()
        out3.append(copy)
    for copy in pairs + out2:
        copy.wait_send()
    for copy in out3:
        copy.wait_recv()
    scale = 1.0 / math.sqrt(131072)
    tiles = []
    for d in range(NG):
        first = fold[plane % NG] if d == 0 else r3[d - 1]
        tiles.append((first + r3[d + NG - 1]) * scale)
    rows = []
    for k in range(4):
        halves = []
        for h in range(2):
            piece = None
            for j in range(4):
                moved = tiles[4 * h + j]
                if j != k:
                    moved = pltpu.roll(moved, (j - k) % 4 * 32, 1)
                piece = moved if piece is None else jnp.where(quarter == j, moved, piece)
            halves.append(piece)
        rows.append(jnp.concatenate(halves, axis=1))
    g[xy] = jnp.concatenate(rows, axis=0).astype(jnp.bfloat16)

    out4 = {}
    for d in FAR_XY:
        out4[d] = pltpu.make_async_remote_copy(
            src_ref=g.at[xy], dst_ref=g.at[xy], send_sem=send4.at[d - 1], recv_sem=recv4.at[d - 1],
            device_id=xy_device(d, core), device_id_type=MESH)
        out4[d].start()

    for copy in out3:
        copy.wait_send()

    wanted = 8 * px + 4 * zh + py
    holder = wanted // NXY == core
    where = wanted % NXY
    hand = pltpu.make_async_remote_copy(
        src_ref=g.at[where], dst_ref=rows32, send_sem=send5, recv_sem=recv5,
        device_id=sibling, device_id_type=MESH)
    shift = (px - where // NY + NX) % NX

    @pl.when(holder & (shift == 0))
    def _():
        hand.start()

    for step in (1, 3, 2):
        out4[NY * step].wait_recv()

        @pl.when(holder & (shift == step))
        def _():
            hand.start()

    @pl.when(holder)
    def _():
        hand.wait_send()
        rows32[...] = g[where]

    @pl.when(jnp.logical_not(holder))
    def _():
        hand.wait_recv()

    concept = lax.broadcasted_iota(jnp.int32, (16, 256), 1) % 32 // 8

    def left_of(part):
        own = rows32[pl.ds(pl.multiple_of(16 * part, 16), 16), :]
        return [jnp.where(concept == k, own, jnp.zeros_like(own)) for k in range(4)]

    left = jnp.concatenate(left_of(1 - core) + left_of(core), axis=0)
    swaps = []
    for step in (0, 1, 3, 2):
        for dy in (1, 3, 2):
            out4[NY * step + dy].wait_recv()
        came = (px - step + NX) % NX
        quarter_rows = g[pl.ds(4 * came, 4)].reshape(128, 256)
        found = lax.dot_general(left, quarter_rows, (((1,), (1,)), ((), ())), preferred_element_type=jnp.float32)
        found = found * (C / 1024)
        give[step] = found[:64]
        swap = pltpu.make_async_remote_copy(
            src_ref=give.at[step], dst_ref=take.at[step], send_sem=send6.at[step], recv_sem=recv6.at[step],
            device_id=sibling, device_id_type=MESH)
        swap.start()
        swaps.append((swap, step, came))
        at = pl.multiple_of(512 * core + 128 * came, 128)
        out_ref[:, :, pl.ds(at, 128)] = found[64:].reshape(4, 16, 128)
    for copy in out4.values():
        copy.wait_send()
    for swap, step, came in swaps:
        swap.wait_recv()
        at = pl.multiple_of(512 * (1 - core) + 128 * came, 128)
        out_ref[:, :, pl.ds(at, 128)] = take[step].reshape(4, 16, 128)
    for swap, step, came in swaps:
        swap.wait_send()


def body(features, signs, columns, labels):
    args = features, signs.reshape(1, -1), columns.reshape(8, 128), labels.reshape(1, 128)
    vmem = pl.BlockSpec(memory_space=pltpu.VMEM)
    dma = pltpu.SemaphoreType.DMA
    return pl.pallas_call(
        kernel,
        out_shape=jax.ShapeDtypeStruct((4, 16, 1024), jnp.float32),
        in_specs=[pl.BlockSpec(memory_space=pltpu.HBM)] * 4,
        out_specs=vmem,
        scratch_shapes=[
            pltpu.VMEM((128, 2048), jnp.bfloat16),
            pltpu.VMEM((1, 2048), jnp.int32),
            pltpu.VMEM((8, 128), jnp.int32),
            pltpu.VMEM((1, 128), jnp.int32),
            pltpu.VMEM((256, 1024), jnp.bfloat16),
            pltpu.VMEM((8, 128, 1024), jnp.bfloat16),
            pltpu.VMEM((8, 128, 128), jnp.float32),
            pltpu.VMEM((32, 32, 128), jnp.float32),
            pltpu.VMEM((16, 32, 128), jnp.float32),
            pltpu.VMEM((15, 32, 128), jnp.float32),
            pltpu.VMEM((8, 8, 128), jnp.float32),
            pltpu.VMEM((15, 8, 128), jnp.float32),
            pltpu.VMEM((16, 32, 256), jnp.bfloat16),
            pltpu.VMEM((32, 256), jnp.bfloat16),
            pltpu.VMEM((4, 64, 128), jnp.float32),
            pltpu.VMEM((4, 64, 128), jnp.float32),
            dma((11,)), dma((4,)), dma((4,)), dma((15,)), dma((15,)), dma((15,)), dma((15,)), dma((15,)), dma((15,)),
            dma, dma, dma((4,)), dma((4,)), pltpu.SemaphoreType.REGULAR, pltpu.SemaphoreType.REGULAR,
        ],
        compiler_params=pltpu.CompilerParams(
            collective_id=0, has_side_effects=True, vmem_limit_bytes=40 * 1024 * 1024),
    )(*[pltpu.with_memory_space_constraint(arg, pltpu.HBM) for arg in args])


def solution(mesh):
    in_specs = (P("tok", "feat"), P("feat"), P(), P("tok", None))
    out_specs = P("tok", "feat", None)
    return jax.shard_map(body, mesh=mesh, in_specs=in_specs, out_specs=out_specs, check_vma=False)
```

```python
import math

import jax
import jax.numpy as jnp
from jax import lax
from jax.experimental import pallas as pl
from jax.experimental.pallas import tpu as pltpu
from jax.sharding import PartitionSpec as P

C = 32
MESH = pl.DeviceIdType.MESH
NX, NH, NY, NC, NG = 4, 2, 4, 2, 8
NXY = NX * NY
NZ = NH * NG


FAR_XY = (10, 6, 14, 9, 11, 2, 8, 5, 7, 13, 15, 1, 3, 4, 12)
STEPS = (2, 1, 3, 0)
FAR_Z = (8, 7, 9, 6, 10, 5, 11, 4, 12, 3, 13, 2, 14, 1, 15)


def kernel(x_hbm, sg_hbm, col_hbm, lab_hbm, out_ref, x_ref, sg_ref, col_ref, lab_ref, xs, s, flip, y, r1, r2, fold, r3, g,
           rows32, give, take, load, send1, recv1, send2, recv2, send3, recv3, send4, recv4, send5, recv5, send6, recv6,
           both_here, all_here, line_here):
    loads = [pltpu.make_async_copy(*pair, load.at[i]) for i, pair in enumerate(
        [(col_hbm, col_ref), (sg_hbm, sg_ref), (lab_hbm, lab_ref)]
        + [(x_hbm.at[pl.ds(16 * k, 16)], x_ref.at[pl.ds(16 * k, 16)]) for k in range(8)])]
    for copy in loads:
        copy.start()
    f = lax.axis_index("feat")
    tok = lax.axis_index("tok")
    core = f % NC
    py = f // NC % NY
    zh = f // (NC * NY) % NH
    px = f // (NC * NY * NH)
    xy = px * NY + py
    plane = zh * NG + tok

    def feat_of(qx, qh, qy, qc):
        return ((qx * NH + qh) * NY + qy) * NC + qc

    sibling = {"feat": feat_of(px, zh, py, 1 - core), "tok": tok}

    def xy_at(d):
        return (px + d // NY) % NX, (py + d % NY) % NY

    def xy_device(d, c):
        qx, qy = xy_at(d)
        return {"feat": feat_of(qx, zh, qy, c), "tok": tok}

    def z_device(d, c):
        other = (plane + d) % NZ
        return {"feat": feat_of(px, other // NG, py, c), "tok": other % NG}

    def signal(sem, device):
        pl.semaphore_signal(sem, inc=1, device_id=device, device_id_type=MESH)

    barrier = pltpu.get_barrier_semaphore()
    hub = (px // 2) * (py // 2) == 1
    hub_x, hub_y = 3 - (px + 1) // 2 % 2, 3 - (py + 1) // 2 % 2
    plain = jnp.logical_not(hub)

    @pl.when((core == 0) & plain | (core == 1) & hub)
    def _():
        signal(barrier, sibling)

    for d in FAR_XY:
        signal(barrier, xy_device(d, 0))
    for d in FAR_Z:
        other = (plane + d) % NZ
        signal(barrier, {"feat": feat_of(hub_x, other // NG, hub_y, 1), "tok": other % NG})

    @pl.when((core == 1) & plain)
    def _():
        pl.semaphore_wait(barrier, 1)
        signal(both_here, sibling)

    loads[0].wait()
    lane = lax.broadcasted_iota(jnp.int32, (128, 128), 1)
    kept_at = col_ref[...]
    high = kept_at >> 11 & f
    for shift in (4, 2, 1):
        high = high ^ high >> shift
    code = kept_at & 127 | (high & 1) << 7 | (kept_at & 1920) << 1
    for i in range(8):
        c = jnp.broadcast_to(code[i:i + 1, :], (128, 128)).T
        v = c & (lane | 128)
        for shift in (4, 2, 1):
            v = v ^ v >> shift
        parts = [(1 - 2 * (v & 1)).astype(jnp.float32).astype(jnp.bfloat16)]
        for bit in range(3):
            turn = (1 - 2 * (c >> 8 + bit & 1)).astype(jnp.float32).astype(jnp.bfloat16)
            parts = parts + [part * turn for part in parts]
        for block in range(8):
            s[i, :, 128 * block:128 * block + 128] = parts[block]
        flip[i] = (1 - 2 * (c >> 11 & 1)).astype(jnp.float32)

    for copy in loads[1:]:
        copy.wait()
    sign = sg_ref[...].astype(jnp.float32).astype(jnp.bfloat16)
    for h in range(2):
        xs[128 * h:128 * h + 128, :] = x_ref[:, 1024 * h:1024 * h + 1024] * sign[:, 1024 * h:1024 * h + 1024]

    def half_of(c):
        kept = s[pl.ds(4 * c, 4)].reshape(512, 1024)
        found = lax.dot_general(kept, xs[...], (((1,), (1,)), ((), ())), preferred_element_type=jnp.float32)
        found = found[:, :128] + found[:, 128:] * flip[pl.ds(4 * c, 4)].reshape(512, 128)
        y[pl.ds(NXY * c, NXY)] = found.reshape(NXY, 32, 128)

    half_of(1 - core)

    @pl.when((core == 0) & plain)
    def _():
        pl.semaphore_wait(both_here, 1)

    @pl.when((core == 0) & hub)
    def _():
        pl.semaphore_wait(barrier, 2 * (NXY - 1) + 1)
        signal(all_here, sibling)

    @pl.when((core == 1) & hub)
    def _():
        pl.semaphore_wait(all_here, 1)

    pairs = []
    for k, step in enumerate(STEPS):
        there = 4 * ((px + step) % NX)
        pairs.append(pltpu.make_async_remote_copy(
            src_ref=y.at[pl.ds(NXY * (1 - core) + there, 4)], dst_ref=r1.at[pl.ds(there, 4)],
            send_sem=send1.at[k], recv_sem=recv1.at[k], device_id=sibling, device_id_type=MESH))
        pairs[k].start()
    half_of(core)

    row = jnp.broadcast_to(lab_ref[...], (128, 128))
    col = row.T
    above = lax.broadcasted_iota(jnp.int32, (128, 128), 0)
    earlier = jnp.where((row == col) & (lane < above), 1.0, 0.0)
    rank = jnp.sum(earlier, axis=1, keepdims=True)
    slot = col.astype(jnp.float32) * 8.0 + rank
    within = (lane % 32).astype(jnp.float32)
    spread = jnp.concatenate(
        [jnp.where(slot == within + 32.0 * q, 1.0, 0.0).astype(jnp.bfloat16) for q in range(NG)], axis=1)

    @pl.when((core == 0) & plain)
    def _():
        pl.semaphore_wait(barrier, 2 * (NXY - 1))
        signal(all_here, sibling)

    @pl.when((core == 1) & plain)
    def _():
        pl.semaphore_wait(all_here, 1)

    out2 = []
    for k, step in enumerate(STEPS):
        pairs[k].wait_recv()
        for d in [NY * step + dy for dy in (2, 1, 3, 0) if step or dy]:
            qx, qy = xy_at(d)
            there = qx * NY + qy
            mine = NXY * core + there
            y[mine] = y[mine] + r1[there]
            copy = pltpu.make_async_remote_copy(
                src_ref=y.at[mine], dst_ref=r2.at[d - 1], send_sem=send2.at[d - 1], recv_sem=recv2.at[d - 1],
                device_id=xy_device(d, core), device_id_type=MESH)
            copy.start()
            out2.append(copy)
    total = y[NXY * core + xy] + r1[xy]


    @pl.when((core == 1) & hub)
    def _():
        pl.semaphore_wait(barrier, 8 * (NZ - 1))
        signal(line_here, sibling)
        for qx, qy in ((3 - px, 3 - py), (3 - px, py), (px, 3 - py)):
            for c in range(NC):
                signal(line_here, {"feat": feat_of(qx, zh, qy, c), "tok": tok})

    for copy in out2:
        copy.wait_recv()
    for d in range(1, NXY):
        total = total + r2[d - 1]

    hi = total.astype(jnp.bfloat16)
    rest = total - hi.astype(jnp.float32)
    mid = rest.astype(jnp.bfloat16)
    low = (rest - mid.astype(jnp.float32)).astype(jnp.bfloat16)
    picked = jnp.dot(jnp.concatenate([hi, mid, low], axis=0), spread, preferred_element_type=jnp.float32)
    picked = picked[0:32] + picked[32:64] + picked[64:96]
    quarter = lax.broadcasted_iota(jnp.int32, (8, 128), 1) // 32
    for q in range(NG):
        tile = picked[0:8, 128 * q:128 * q + 128]
        for k in range(1, 4):
            tile = jnp.where(quarter == k, picked[8 * k:8 * k + 8, 128 * q:128 * q + 128], tile)
        fold[q] = tile

    @pl.when((core == 0) | plain)
    def _():
        pl.semaphore_wait(line_here, 1)

    out3 = []
    for d in FAR_Z:
        copy = pltpu.make_async_remote_copy(
            src_ref=fold.at[(plane + d) % NG], dst_ref=r3.at[d - 1], send_sem=send3.at[d - 1],
            recv_sem=recv3.at[d - 1], device_id=z_device(d, core), device_id_type=MESH)
        copy.start()
        out3.append(copy)
    for copy in pairs + out2:
        copy.wait_send()
    for copy in out3:
        copy.wait_recv()
    scale = 1.0 / math.sqrt(131072)
    tiles = []
    for d in range(NG):
        first = fold[plane % NG] if d == 0 else r3[d - 1]
        tiles.append((first + r3[d + NG - 1]) * scale)
    rows = []
    for k in range(4):
        halves = []
        for h in range(2):
            piece = None
            for j in range(4):
                moved = tiles[4 * h + j]
                if j != k:
                    moved = pltpu.roll(moved, (j - k) % 4 * 32, 1)
                piece = moved if piece is None else jnp.where(quarter == j, moved, piece)
            halves.append(piece)
        rows.append(jnp.concatenate(halves, axis=1))
    g[xy] = jnp.concatenate(rows, axis=0).astype(jnp.bfloat16)

    out4 = {}
    for d in FAR_XY:
        out4[d] = pltpu.make_async_remote_copy(
            src_ref=g.at[xy], dst_ref=g.at[xy], send_sem=send4.at[d - 1], recv_sem=recv4.at[d - 1],
            device_id=xy_device(d, core), device_id_type=MESH)
        out4[d].start()

    for copy in out3:
        copy.wait_send()

    wanted = 8 * px + 4 * zh + py
    holder = wanted // NXY == core
    where = wanted % NXY
    hand = pltpu.make_async_remote_copy(
        src_ref=g.at[where], dst_ref=rows32, send_sem=send5, recv_sem=recv5,
        device_id=sibling, device_id_type=MESH)
    shift = (px - where // NY + NX) % NX

    @pl.when(holder & (shift == 0))
    def _():
        hand.start()

    for step in (1, 3, 2):
        out4[NY * step].wait_recv()

        @pl.when(holder & (shift == step))
        def _():
            hand.start()

    @pl.when(holder)
    def _():
        hand.wait_send()
        rows32[...] = g[where]

    @pl.when(jnp.logical_not(holder))
    def _():
        hand.wait_recv()

    concept = lax.broadcasted_iota(jnp.int32, (16, 256), 1) % 32 // 8

    def left_of(part):
        own = rows32[pl.ds(pl.multiple_of(16 * part, 16), 16), :]
        return [jnp.where(concept == k, own, jnp.zeros_like(own)) for k in range(4)]

    left = jnp.concatenate(left_of(1 - core) + left_of(core), axis=0)
    swaps = []
    for step in (0, 1, 3, 2):
        for dy in (1, 3, 2):
            out4[NY * step + dy].wait_recv()
        came = (px - step + NX) % NX
        quarter_rows = g[pl.ds(4 * came, 4)].reshape(128, 256)
        found = lax.dot_general(left, quarter_rows, (((1,), (1,)), ((), ())), preferred_element_type=jnp.float32)
        found = found * (C / 1024)
        give[step] = found[:64]
        swap = pltpu.make_async_remote_copy(
            src_ref=give.at[step], dst_ref=take.at[step], send_sem=send6.at[step], recv_sem=recv6.at[step],
            device_id=sibling, device_id_type=MESH)
        swap.start()
        swaps.append((swap, step, came))
        at = pl.multiple_of(512 * core + 128 * came, 128)
        out_ref[:, :, pl.ds(at, 128)] = found[64:].reshape(4, 16, 128)
    for copy in out4.values():
        copy.wait_send()
    for swap, step, came in swaps:
        swap.wait_recv()
        at = pl.multiple_of(512 * (1 - core) + 128 * came, 128)
        out_ref[:, :, pl.ds(at, 128)] = take[step].reshape(4, 16, 128)
    for swap, step, came in swaps:
        swap.wait_send()


def body(features, signs, columns, labels):
    args = features, signs.reshape(1, -1), columns.reshape(8, 128), labels.reshape(1, 128)
    vmem = pl.BlockSpec(memory_space=pltpu.VMEM)
    dma = pltpu.SemaphoreType.DMA
    return pl.pallas_call(
        kernel,
        out_shape=jax.ShapeDtypeStruct((4, 16, 1024), jnp.float32),
        in_specs=[pl.BlockSpec(memory_space=pltpu.HBM)] * 4,
        out_specs=vmem,
        scratch_shapes=[
            pltpu.VMEM((128, 2048), jnp.bfloat16),
            pltpu.VMEM((1, 2048), jnp.int32),
            pltpu.VMEM((8, 128), jnp.int32),
            pltpu.VMEM((1, 128), jnp.int32),
            pltpu.VMEM((256, 1024), jnp.bfloat16),
            pltpu.VMEM((8, 128, 1024), jnp.bfloat16),
            pltpu.VMEM((8, 128, 128), jnp.float32),
            pltpu.VMEM((32, 32, 128), jnp.float32),
            pltpu.VMEM((16, 32, 128), jnp.float32),
            pltpu.VMEM((15, 32, 128), jnp.float32),
            pltpu.VMEM((8, 8, 128), jnp.float32),
            pltpu.VMEM((15, 8, 128), jnp.float32),
            pltpu.VMEM((16, 32, 256), jnp.bfloat16),
            pltpu.VMEM((32, 256), jnp.bfloat16),
            pltpu.VMEM((4, 64, 128), jnp.float32),
            pltpu.VMEM((4, 64, 128), jnp.float32),
            dma((11,)), dma((4,)), dma((4,)), dma((15,)), dma((15,)), dma((15,)), dma((15,)), dma((15,)), dma((15,)),
            dma, dma, dma((4,)), dma((4,)), pltpu.SemaphoreType.REGULAR, pltpu.SemaphoreType.REGULAR,
            pltpu.SemaphoreType.REGULAR,
        ],
        compiler_params=pltpu.CompilerParams(
            collective_id=0, has_side_effects=True, vmem_limit_bytes=40 * 1024 * 1024),
    )(*[pltpu.with_memory_space_constraint(arg, pltpu.HBM) for arg in args])


def solution(mesh):
    in_specs = (P("tok", "feat"), P("feat"), P(), P("tok", None))
    out_specs = P("tok", "feat", None)
    return jax.shard_map(body, mesh=mesh, in_specs=in_specs, out_specs=out_specs, check_vma=False)
```

```python
import math

import jax
import jax.numpy as jnp
from jax import lax
from jax.experimental import pallas as pl
from jax.experimental.pallas import tpu as pltpu
from jax.sharding import PartitionSpec as P

C = 32
MESH = pl.DeviceIdType.MESH
NX, NH, NY, NC, NG = 4, 2, 4, 2, 8
NXY = NX * NY
NZ = NH * NG


FAR_XY = (10, 6, 14, 9, 11, 2, 8, 5, 7, 13, 15, 1, 3, 4, 12)
STEPS = (2, 1, 3, 0)
FAR_Z = (8, 7, 9, 6, 10, 5, 11, 4, 12, 3, 13, 2, 14, 1, 15)


def kernel(x_hbm, sg_hbm, col_hbm, lab_hbm, out_ref, x_ref, sg_ref, col_ref, lab_ref, xs, s, flip, y, r1, r2, fold, r3, g,
           rows32, give, take, load, send1, recv1, send2, recv2, send3, recv3, send4, recv4, send5, recv5, send6, recv6,
           both_here, all_here, line_here):
    loads = [pltpu.make_async_copy(*pair, load.at[i]) for i, pair in enumerate(
        [(col_hbm, col_ref), (sg_hbm, sg_ref), (lab_hbm, lab_ref)]
        + [(x_hbm.at[pl.ds(16 * k, 16)], x_ref.at[pl.ds(16 * k, 16)]) for k in range(8)])]
    f = lax.axis_index("feat")
    tok = lax.axis_index("tok")
    core = f % NC
    py = f // NC % NY
    zh = f // (NC * NY) % NH
    px = f // (NC * NY * NH)
    xy = px * NY + py
    plane = zh * NG + tok

    def feat_of(qx, qh, qy, qc):
        return ((qx * NH + qh) * NY + qy) * NC + qc

    sibling = {"feat": feat_of(px, zh, py, 1 - core), "tok": tok}

    def xy_at(d):
        return (px + d // NY) % NX, (py + d % NY) % NY

    def xy_device(d, c):
        qx, qy = xy_at(d)
        return {"feat": feat_of(qx, zh, qy, c), "tok": tok}

    def z_device(d, c):
        other = (plane + d) % NZ
        return {"feat": feat_of(px, other // NG, py, c), "tok": other % NG}

    def signal(sem, device):
        pl.semaphore_signal(sem, inc=1, device_id=device, device_id_type=MESH)

    barrier = pltpu.get_barrier_semaphore()
    hub = (px // 2) * (py // 2) == 1
    hub_x, hub_y = 3 - (px + 1) // 2 % 2, 3 - (py + 1) // 2 % 2
    plain = jnp.logical_not(hub)

    for d in FAR_XY:
        signal(barrier, xy_device(d, 0))

    @pl.when((core == 0) & plain | (core == 1) & hub)
    def _():
        signal(barrier, sibling)

    for copy in loads:
        copy.start()
    for d in FAR_Z:
        other = (plane + d) % NZ
        signal(barrier, {"feat": feat_of(hub_x, other // NG, hub_y, 1), "tok": other % NG})

    @pl.when((core == 1) & plain)
    def _():
        pl.semaphore_wait(barrier, 1)
        signal(both_here, sibling)

    loads[0].wait()
    lane = lax.broadcasted_iota(jnp.int32, (128, 128), 1)
    kept_at = col_ref[...]
    high = kept_at >> 11 & f
    for shift in (4, 2, 1):
        high = high ^ high >> shift
    code = kept_at & 127 | (high & 1) << 7 | (kept_at & 1920) << 1
    for i in range(8):
        c = jnp.broadcast_to(code[i:i + 1, :], (128, 128)).T
        v = c & (lane | 128)
        for shift in (4, 2, 1):
            v = v ^ v >> shift
        parts = [(1 - 2 * (v & 1)).astype(jnp.float32).astype(jnp.bfloat16)]
        for bit in range(3):
            turn = (1 - 2 * (c >> 8 + bit & 1)).astype(jnp.float32).astype(jnp.bfloat16)
            parts = parts + [part * turn for part in parts]
        for block in range(8):
            s[i, :, 128 * block:128 * block + 128] = parts[block]
        flip[i] = (1 - 2 * (c >> 11 & 1)).astype(jnp.float32)

    for copy in loads[1:]:
        copy.wait()
    sign = sg_ref[...].astype(jnp.float32).astype(jnp.bfloat16)
    for h in range(2):
        xs[128 * h:128 * h + 128, :] = x_ref[:, 1024 * h:1024 * h + 1024] * sign[:, 1024 * h:1024 * h + 1024]

    def half_of(c):
        kept = s[pl.ds(4 * c, 4)].reshape(512, 1024)
        found = lax.dot_general(kept, xs[...], (((1,), (1,)), ((), ())), preferred_element_type=jnp.float32)
        found = found[:, :128] + found[:, 128:] * flip[pl.ds(4 * c, 4)].reshape(512, 128)
        y[pl.ds(NXY * c, NXY)] = found.reshape(NXY, 32, 128)

    half_of(1 - core)

    @pl.when((core == 0) & plain)
    def _():
        pl.semaphore_wait(both_here, 1)

    @pl.when((core == 0) & hub)
    def _():
        pl.semaphore_wait(barrier, 2 * (NXY - 1) + 1)
        signal(all_here, sibling)

    @pl.when((core == 1) & hub)
    def _():
        pl.semaphore_wait(all_here, 1)

    pairs = []
    for k, step in enumerate(STEPS):
        there = 4 * ((px + step) % NX)
        pairs.append(pltpu.make_async_remote_copy(
            src_ref=y.at[pl.ds(NXY * (1 - core) + there, 4)], dst_ref=r1.at[pl.ds(there, 4)],
            send_sem=send1.at[k], recv_sem=recv1.at[k], device_id=sibling, device_id_type=MESH))
        pairs[k].start()
    half_of(core)

    row = jnp.broadcast_to(lab_ref[...], (128, 128))
    col = row.T
    above = lax.broadcasted_iota(jnp.int32, (128, 128), 0)
    earlier = jnp.where((row == col) & (lane < above), 1.0, 0.0)
    rank = jnp.sum(earlier, axis=1, keepdims=True)
    slot = col.astype(jnp.float32) * 8.0 + rank
    at = lane.astype(jnp.float32)
    spread = jnp.concatenate(
        [jnp.where(slot == at + 128.0 * q, 1.0, 0.0).astype(jnp.bfloat16) for q in range(2)], axis=1)

    for copy in pairs:
        copy.wait_recv()
    own = pl.ds(NXY * core, NXY)
    y[own] = y[own] + r1[...]

    @pl.when((core == 0) & plain)
    def _():
        pl.semaphore_wait(barrier, 2 * (NXY - 1))
        signal(all_here, sibling)

    @pl.when((core == 1) & plain)
    def _():
        pl.semaphore_wait(all_here, 1)

    out2 = []
    for k, step in enumerate(STEPS):
        for d in [NY * step + dy for dy in (2, 1, 3, 0) if step or dy]:
            qx, qy = xy_at(d)
            there = qx * NY + qy
            mine = NXY * core + there
            copy = pltpu.make_async_remote_copy(
                src_ref=y.at[mine], dst_ref=r2.at[d - 1], send_sem=send2.at[d - 1], recv_sem=recv2.at[d - 1],
                device_id=xy_device(d, core), device_id_type=MESH)
            copy.start()
            out2.append(copy)
    total = y[NXY * core + xy]


    @pl.when((core == 1) & hub)
    def _():
        pl.semaphore_wait(barrier, 8 * (NZ - 1))
        signal(line_here, sibling)
        for qx, qy in ((3 - px, 3 - py), (3 - px, py), (px, 3 - py)):
            for c in range(NC):
                signal(line_here, {"feat": feat_of(qx, zh, qy, c), "tok": tok})

    for copy in out2:
        copy.wait_recv()
    for d in range(1, NXY):
        total = total + r2[d - 1]

    hi = total.astype(jnp.bfloat16)
    rest = total - hi.astype(jnp.float32)
    mid = rest.astype(jnp.bfloat16)
    low = (rest - mid.astype(jnp.float32)).astype(jnp.bfloat16)
    picked = jnp.dot(jnp.concatenate([hi, mid, low], axis=0), spread, preferred_element_type=jnp.float32)
    picked = picked[0:32] + picked[32:64] + picked[64:96]
    quarter = lax.broadcasted_iota(jnp.int32, (8, 128), 1) // 32
    for q in range(NG):
        tile = None
        for k in range(4):
            part = picked[8 * k:8 * k + 8, 128 * (q // 4):128 * (q // 4) + 128]
            if q % 4 != k:
                part = pltpu.roll(part, (k - q % 4) % 4 * 32, 1)
            tile = part if tile is None else jnp.where(quarter == k, part, tile)
        fold[q] = tile

    @pl.when((core == 0) | plain)
    def _():
        pl.semaphore_wait(line_here, 1)

    out3 = []
    for d in FAR_Z:
        copy = pltpu.make_async_remote_copy(
            src_ref=fold.at[(plane + d) % NG], dst_ref=r3.at[d - 1], send_sem=send3.at[d - 1],
            recv_sem=recv3.at[d - 1], device_id=z_device(d, core), device_id_type=MESH)
        copy.start()
        out3.append(copy)
    for copy in pairs + out2:
        copy.wait_send()
    for copy in out3:
        copy.wait_recv()
    scale = 1.0 / math.sqrt(131072)
    tiles = []
    for d in range(NG):
        first = fold[plane % NG] if d == 0 else r3[d - 1]
        tiles.append((first + r3[d + NG - 1]) * scale)
    rows = []
    for k in range(4):
        halves = []
        for h in range(2):
            piece = None
            for j in range(4):
                moved = tiles[4 * h + j]
                if j != k:
                    moved = pltpu.roll(moved, (j - k) % 4 * 32, 1)
                piece = moved if piece is None else jnp.where(quarter == j, moved, piece)
            halves.append(piece)
        rows.append(jnp.concatenate(halves, axis=1))
    g[xy] = jnp.concatenate(rows, axis=0).astype(jnp.bfloat16)

    out4 = {}
    for d in FAR_XY:
        out4[d] = pltpu.make_async_remote_copy(
            src_ref=g.at[xy], dst_ref=g.at[xy], send_sem=send4.at[d - 1], recv_sem=recv4.at[d - 1],
            device_id=xy_device(d, core), device_id_type=MESH)
        out4[d].start()

    for copy in out3:
        copy.wait_send()

    wanted = 8 * px + 4 * zh + py
    holder = wanted // NXY == core
    where = wanted % NXY
    hand = pltpu.make_async_remote_copy(
        src_ref=g.at[where], dst_ref=rows32, send_sem=send5, recv_sem=recv5,
        device_id=sibling, device_id_type=MESH)
    shift = (px - where // NY + NX) % NX

    @pl.when(holder & (shift == 0))
    def _():
        hand.start()

    for step in (1, 3, 2):
        out4[NY * step].wait_recv()

        @pl.when(holder & (shift == step))
        def _():
            hand.start()

    @pl.when(holder)
    def _():
        rows32[...] = g[where]

    @pl.when(jnp.logical_not(holder))
    def _():
        hand.wait_recv()

    concept = lax.broadcasted_iota(jnp.int32, (16, 256), 1) % 32 // 8

    def left_of(part):
        own = rows32[pl.ds(pl.multiple_of(16 * part, 16), 16), :]
        return [jnp.where(concept == k, own, jnp.zeros_like(own)) for k in range(4)]

    left = jnp.concatenate(left_of(1 - core) + left_of(core), axis=0)
    swaps = []
    for step in (0, 1, 3, 2):
        for dy in (1, 3, 2):
            out4[NY * step + dy].wait_recv()
        came = (px - step + NX) % NX
        quarter_rows = g[pl.ds(4 * came, 4)].reshape(128, 256)
        found = lax.dot_general(left, quarter_rows, (((1,), (1,)), ((), ())), preferred_element_type=jnp.float32)
        found = found * (C / 1024)
        give[step] = found[:64]
        swap = pltpu.make_async_remote_copy(
            src_ref=give.at[step], dst_ref=take.at[step], send_sem=send6.at[step], recv_sem=recv6.at[step],
            device_id=sibling, device_id_type=MESH)
        swap.start()
        swaps.append((swap, step, came))
        at = pl.multiple_of(512 * core + 128 * came, 128)
        out_ref[:, :, pl.ds(at, 128)] = found[64:].reshape(4, 16, 128)
    for copy in out4.values():
        copy.wait_send()
    for swap, step, came in swaps:
        swap.wait_recv()
        at = pl.multiple_of(512 * (1 - core) + 128 * came, 128)
        out_ref[:, :, pl.ds(at, 128)] = take[step].reshape(4, 16, 128)
    for swap, step, came in swaps:
        swap.wait_send()

    @pl.when(holder)
    def _():
        hand.wait_send()


def body(features, signs, columns, labels):
    args = features, signs.reshape(1, -1), columns.reshape(8, 128), labels.reshape(1, 128)
    vmem = pl.BlockSpec(memory_space=pltpu.VMEM)
    dma = pltpu.SemaphoreType.DMA
    return pl.pallas_call(
        kernel,
        out_shape=jax.ShapeDtypeStruct((4, 16, 1024), jnp.float32),
        in_specs=[pl.BlockSpec(memory_space=pltpu.HBM)] * 4,
        out_specs=vmem,
        scratch_shapes=[
            pltpu.VMEM((128, 2048), jnp.bfloat16),
            pltpu.VMEM((1, 2048), jnp.int32),
            pltpu.VMEM((8, 128), jnp.int32),
            pltpu.VMEM((1, 128), jnp.int32),
            pltpu.VMEM((256, 1024), jnp.bfloat16),
            pltpu.VMEM((8, 128, 1024), jnp.bfloat16),
            pltpu.VMEM((8, 128, 128), jnp.float32),
            pltpu.VMEM((32, 32, 128), jnp.float32),
            pltpu.VMEM((16, 32, 128), jnp.float32),
            pltpu.VMEM((15, 32, 128), jnp.float32),
            pltpu.VMEM((8, 8, 128), jnp.float32),
            pltpu.VMEM((15, 8, 128), jnp.float32),
            pltpu.VMEM((16, 32, 256), jnp.bfloat16),
            pltpu.VMEM((32, 256), jnp.bfloat16),
            pltpu.VMEM((4, 64, 128), jnp.float32),
            pltpu.VMEM((4, 64, 128), jnp.float32),
            dma((11,)), dma((4,)), dma((4,)), dma((15,)), dma((15,)), dma((15,)), dma((15,)), dma((15,)), dma((15,)),
            dma, dma, dma((4,)), dma((4,)), pltpu.SemaphoreType.REGULAR, pltpu.SemaphoreType.REGULAR,
            pltpu.SemaphoreType.REGULAR,
        ],
        compiler_params=pltpu.CompilerParams(
            collective_id=0, has_side_effects=True, vmem_limit_bytes=40 * 1024 * 1024),
    )(*[pltpu.with_memory_space_constraint(arg, pltpu.HBM) for arg in args])


def solution(mesh):
    in_specs = (P("tok", "feat"), P("feat"), P(), P("tok", None))
    out_specs = P("tok", "feat", None)
    return jax.shard_map(body, mesh=mesh, in_specs=in_specs, out_specs=out_specs, check_vma=False)
```

```python
import math

import jax
import jax.numpy as jnp
from jax import lax
from jax.experimental import pallas as pl
from jax.experimental.pallas import tpu as pltpu
from jax.sharding import PartitionSpec as P

C = 32
MESH = pl.DeviceIdType.MESH
NX, NH, NY, NC, NG = 4, 2, 4, 2, 8
NXY = NX * NY
NZ = NH * NG


FAR_XY = (10, 6, 14, 9, 11, 2, 8, 5, 7, 13, 15, 1, 3, 4, 12)
STEPS = (2, 1, 3, 0)
FAR_Z = (8, 7, 9, 6, 10, 5, 11, 4, 12, 3, 13, 2, 14, 1, 15)


def kernel(x_hbm, sg_hbm, col_hbm, lab_hbm, out_ref, x_ref, sg_ref, col_ref, lab_ref, xs, s, flip, y, r1, r2, fold, r3, g,
           rows32, give, take, load, send1, recv1, send2, recv2, send3, recv3, send4, recv4, send5, recv5, send6, recv6,
           both_here, all_here, line_here):
    loads = [pltpu.make_async_copy(*pair, load.at[i]) for i, pair in enumerate(
        [(col_hbm, col_ref), (sg_hbm, sg_ref), (lab_hbm, lab_ref)]
        + [(x_hbm.at[pl.ds(16 * k, 16)], x_ref.at[pl.ds(16 * k, 16)]) for k in range(8)])]
    for copy in loads:
        copy.start()
    f = lax.axis_index("feat")
    tok = lax.axis_index("tok")
    core = f % NC
    py = f // NC % NY
    zh = f // (NC * NY) % NH
    px = f // (NC * NY * NH)
    xy = px * NY + py
    plane = zh * NG + tok

    def feat_of(qx, qh, qy, qc):
        return ((qx * NH + qh) * NY + qy) * NC + qc

    sibling = {"feat": feat_of(px, zh, py, 1 - core), "tok": tok}

    def xy_at(d):
        return (px + d // NY) % NX, (py + d % NY) % NY

    def xy_device(d, c):
        qx, qy = xy_at(d)
        return {"feat": feat_of(qx, zh, qy, c), "tok": tok}

    def z_device(d, c):
        other = (plane + d) % NZ
        return {"feat": feat_of(px, other // NG, py, c), "tok": other % NG}

    def signal(sem, device):
        pl.semaphore_signal(sem, inc=1, device_id=device, device_id_type=MESH)

    barrier = pltpu.get_barrier_semaphore()
    hub = (px // 2) * (py // 2) == 1
    hub_x, hub_y = 3 - (px + 1) // 2 % 2, 3 - (py + 1) // 2 % 2
    plain = jnp.logical_not(hub)

    @pl.when((core == 0) & plain | (core == 1) & hub)
    def _():
        signal(barrier, sibling)

    for d in FAR_XY:
        signal(barrier, xy_device(d, 0))
    for d in FAR_Z:
        other = (plane + d) % NZ
        signal(barrier, {"feat": feat_of(hub_x, other // NG, hub_y, 1), "tok": other % NG})

    @pl.when((core == 1) & plain)
    def _():
        pl.semaphore_wait(barrier, 1)
        signal(both_here, sibling)

    loads[0].wait()
    lane = lax.broadcasted_iota(jnp.int32, (128, 128), 1)
    kept_at = col_ref[...]
    high = kept_at >> 11 & f
    for shift in (4, 2, 1):
        high = high ^ high >> shift
    col_ref[...] = kept_at & 127 | (high & 1) << 7 | (kept_at & 1920) << 1

    def signs_of(c):
        for n in range(4):
            i = 4 * c + n
            code = jnp.broadcast_to(col_ref[pl.ds(i, 1), :], (128, 128)).T
            v = code & (lane | 128)
            for shift in (4, 2, 1):
                v = v ^ v >> shift
            parts = [(1 - 2 * (v & 1)).astype(jnp.float32).astype(jnp.bfloat16)]
            for bit in range(3):
                turn = (1 - 2 * (code >> 8 + bit & 1)).astype(jnp.float32).astype(jnp.bfloat16)
                parts = parts + [part * turn for part in parts]
            for block in range(8):
                s[i, :, 128 * block:128 * block + 128] = parts[block]
            flip[i] = (1 - 2 * (code >> 11 & 1)).astype(jnp.float32)

    signs_of(1 - core)
    for copy in loads[1:]:
        copy.wait()
    sign = sg_ref[...].astype(jnp.float32).astype(jnp.bfloat16)
    for h in range(2):
        xs[128 * h:128 * h + 128, :] = x_ref[:, 1024 * h:1024 * h + 1024] * sign[:, 1024 * h:1024 * h + 1024]

    def half_of(c):
        kept = s[pl.ds(4 * c, 4)].reshape(512, 1024)
        found = lax.dot_general(kept, xs[...], (((1,), (1,)), ((), ())), preferred_element_type=jnp.float32)
        found = found[:, :128] + found[:, 128:] * flip[pl.ds(4 * c, 4)].reshape(512, 128)
        y[pl.ds(NXY * c, NXY)] = found.reshape(NXY, 32, 128)

    half_of(1 - core)

    @pl.when((core == 0) & plain)
    def _():
        pl.semaphore_wait(both_here, 1)

    @pl.when((core == 0) & hub)
    def _():
        pl.semaphore_wait(barrier, 2 * (NXY - 1) + 1)
        signal(all_here, sibling)

    @pl.when((core == 1) & hub)
    def _():
        pl.semaphore_wait(all_here, 1)

    pairs = []
    for k, step in enumerate(STEPS):
        there = 4 * ((px + step) % NX)
        pairs.append(pltpu.make_async_remote_copy(
            src_ref=y.at[pl.ds(NXY * (1 - core) + there, 4)], dst_ref=r1.at[pl.ds(there, 4)],
            send_sem=send1.at[k], recv_sem=recv1.at[k], device_id=sibling, device_id_type=MESH))
        pairs[k].start()
    signs_of(core)
    half_of(core)

    row = jnp.broadcast_to(lab_ref[...], (128, 128))
    col = row.T
    above = lax.broadcasted_iota(jnp.int32, (128, 128), 0)
    earlier = jnp.where((row == col) & (lane < above), 1.0, 0.0)
    rank = jnp.sum(earlier, axis=1, keepdims=True)
    slot = col.astype(jnp.float32) * 8.0 + rank
    within = (lane % 32).astype(jnp.float32)
    spread = jnp.concatenate(
        [jnp.where(slot == within + 32.0 * q, 1.0, 0.0).astype(jnp.bfloat16) for q in range(NG)], axis=1)

    @pl.when((core == 0) & plain)
    def _():
        pl.semaphore_wait(barrier, 2 * (NXY - 1))
        signal(all_here, sibling)

    @pl.when((core == 1) & plain)
    def _():
        pl.semaphore_wait(all_here, 1)

    out2 = []
    for k, step in enumerate(STEPS):
        pairs[k].wait_recv()
        for d in [NY * step + dy for dy in (2, 1, 3, 0) if step or dy]:
            qx, qy = xy_at(d)
            there = qx * NY + qy
            mine = NXY * core + there
            y[mine] = y[mine] + r1[there]
            copy = pltpu.make_async_remote_copy(
                src_ref=y.at[mine], dst_ref=r2.at[d - 1], send_sem=send2.at[d - 1], recv_sem=recv2.at[d - 1],
                device_id=xy_device(d, core), device_id_type=MESH)
            copy.start()
            out2.append(copy)
    total = y[NXY * core + xy] + r1[xy]


    @pl.when((core == 1) & hub)
    def _():
        pl.semaphore_wait(barrier, 8 * (NZ - 1))
        signal(line_here, sibling)
        for qx, qy in ((3 - px, 3 - py), (3 - px, py), (px, 3 - py)):
            for c in range(NC):
                signal(line_here, {"feat": feat_of(qx, zh, qy, c), "tok": tok})

    for copy in out2:
        copy.wait_recv()
    for d in range(1, NXY):
        total = total + r2[d - 1]

    hi = total.astype(jnp.bfloat16)
    rest = total - hi.astype(jnp.float32)
    mid = rest.astype(jnp.bfloat16)
    low = (rest - mid.astype(jnp.float32)).astype(jnp.bfloat16)
    picked = jnp.dot(jnp.concatenate([hi, mid, low], axis=0), spread, preferred_element_type=jnp.float32)
    picked = picked[0:32] + picked[32:64] + picked[64:96]
    quarter = lax.broadcasted_iota(jnp.int32, (8, 128), 1) // 32
    for q in range(NG):
        tile = picked[0:8, 128 * q:128 * q + 128]
        for k in range(1, 4):
            tile = jnp.where(quarter == k, picked[8 * k:8 * k + 8, 128 * q:128 * q + 128], tile)
        fold[q] = tile

    @pl.when((core == 0) | plain)
    def _():
        pl.semaphore_wait(line_here, 1)

    out3 = []
    for d in FAR_Z:
        copy = pltpu.make_async_remote_copy(
            src_ref=fold.at[(plane + d) % NG], dst_ref=r3.at[d - 1], send_sem=send3.at[d - 1],
            recv_sem=recv3.at[d - 1], device_id=z_device(d, core), device_id_type=MESH)
        copy.start()
        out3.append(copy)
    for copy in pairs + out2:
        copy.wait_send()
    for copy in out3:
        copy.wait_recv()
    scale = 1.0 / math.sqrt(131072)
    tiles = []
    for d in range(NG):
        first = fold[plane % NG] if d == 0 else r3[d - 1]
        tiles.append((first + r3[d + NG - 1]) * scale)
    rows = []
    for k in range(4):
        halves = []
        for h in range(2):
            piece = None
            for j in range(4):
                moved = tiles[4 * h + j]
                if j != k:
                    moved = pltpu.roll(moved, (j - k) % 4 * 32, 1)
                piece = moved if piece is None else jnp.where(quarter == j, moved, piece)
            halves.append(piece)
        rows.append(jnp.concatenate(halves, axis=1))
    g[xy] = jnp.concatenate(rows, axis=0).astype(jnp.bfloat16)

    out4 = {}
    for d in FAR_XY:
        out4[d] = pltpu.make_async_remote_copy(
            src_ref=g.at[xy], dst_ref=g.at[xy], send_sem=send4.at[d - 1], recv_sem=recv4.at[d - 1],
            device_id=xy_device(d, core), device_id_type=MESH)
        out4[d].start()

    for copy in out3:
        copy.wait_send()

    wanted = 8 * px + 4 * zh + py
    holder = wanted // NXY == core
    where = wanted % NXY
    hand = pltpu.make_async_remote_copy(
        src_ref=g.at[where], dst_ref=rows32, send_sem=send5, recv_sem=recv5,
        device_id=sibling, device_id_type=MESH)
    shift = (px - where // NY + NX) % NX

    @pl.when(holder & (shift == 0))
    def _():
        hand.start()

    for step in (1, 3, 2):
        out4[NY * step].wait_recv()

        @pl.when(holder & (shift == step))
        def _():
            hand.start()

    @pl.when(holder)
    def _():
        hand.wait_send()
        rows32[...] = g[where]

    @pl.when(jnp.logical_not(holder))
    def _():
        hand.wait_recv()

    concept = lax.broadcasted_iota(jnp.int32, (16, 256), 1) % 32 // 8

    def left_of(part):
        own = rows32[pl.ds(pl.multiple_of(16 * part, 16), 16), :]
        return [jnp.where(concept == k, own, jnp.zeros_like(own)) for k in range(4)]

    left = jnp.concatenate(left_of(1 - core) + left_of(core), axis=0)
    swaps = []
    for step in (0, 1, 3, 2):
        for dy in (1, 3, 2):
            out4[NY * step + dy].wait_recv()
        came = (px - step + NX) % NX
        quarter_rows = g[pl.ds(4 * came, 4)].reshape(128, 256)
        found = lax.dot_general(left, quarter_rows, (((1,), (1,)), ((), ())), preferred_element_type=jnp.float32)
        found = found * (C / 1024)
        give[step] = found[:64]
        swap = pltpu.make_async_remote_copy(
            src_ref=give.at[step], dst_ref=take.at[step], send_sem=send6.at[step], recv_sem=recv6.at[step],
            device_id=sibling, device_id_type=MESH)
        swap.start()
        swaps.append((swap, step, came))
        at = pl.multiple_of(512 * core + 128 * came, 128)
        out_ref[:, :, pl.ds(at, 128)] = found[64:].reshape(4, 16, 128)
    for copy in out4.values():
        copy.wait_send()
    for swap, step, came in swaps:
        swap.wait_recv()
        at = pl.multiple_of(512 * (1 - core) + 128 * came, 128)
        out_ref[:, :, pl.ds(at, 128)] = take[step].reshape(4, 16, 128)
    for swap, step, came in swaps:
        swap.wait_send()


def body(features, signs, columns, labels):
    args = features, signs.reshape(1, -1), columns.reshape(8, 128), labels.reshape(1, 128)
    vmem = pl.BlockSpec(memory_space=pltpu.VMEM)
    dma = pltpu.SemaphoreType.DMA
    return pl.pallas_call(
        kernel,
        out_shape=jax.ShapeDtypeStruct((4, 16, 1024), jnp.float32),
        in_specs=[pl.BlockSpec(memory_space=pltpu.HBM)] * 4,
        out_specs=vmem,
        scratch_shapes=[
            pltpu.VMEM((128, 2048), jnp.bfloat16),
            pltpu.VMEM((1, 2048), jnp.int32),
            pltpu.VMEM((8, 128), jnp.int32),
            pltpu.VMEM((1, 128), jnp.int32),
            pltpu.VMEM((256, 1024), jnp.bfloat16),
            pltpu.VMEM((8, 128, 1024), jnp.bfloat16),
            pltpu.VMEM((8, 128, 128), jnp.float32),
            pltpu.VMEM((32, 32, 128), jnp.float32),
            pltpu.VMEM((16, 32, 128), jnp.float32),
            pltpu.VMEM((15, 32, 128), jnp.float32),
            pltpu.VMEM((8, 8, 128), jnp.float32),
            pltpu.VMEM((15, 8, 128), jnp.float32),
            pltpu.VMEM((16, 32, 256), jnp.bfloat16),
            pltpu.VMEM((32, 256), jnp.bfloat16),
            pltpu.VMEM((4, 64, 128), jnp.float32),
            pltpu.VMEM((4, 64, 128), jnp.float32),
            dma((11,)), dma((4,)), dma((4,)), dma((15,)), dma((15,)), dma((15,)), dma((15,)), dma((15,)), dma((15,)),
            dma, dma, dma((4,)), dma((4,)), pltpu.SemaphoreType.REGULAR, pltpu.SemaphoreType.REGULAR,
            pltpu.SemaphoreType.REGULAR,
        ],
        compiler_params=pltpu.CompilerParams(
            collective_id=0, has_side_effects=True, vmem_limit_bytes=40 * 1024 * 1024),
    )(*[pltpu.with_memory_space_constraint(arg, pltpu.HBM) for arg in args])


def solution(mesh):
    in_specs = (P("tok", "feat"), P("feat"), P(), P("tok", None))
    out_specs = P("tok", "feat", None)
    return jax.shard_map(body, mesh=mesh, in_specs=in_specs, out_specs=out_specs, check_vma=False)
```
